512 devices in a mesh: gx: 32 (over z, core), gy: 4 (over x), gz: 4 (over y).
Axes of the slice: x: 4, y: 4, z: 16, core: 2. Of those that a mesh axis runs over, the one named last changes fastest.
Arguments:
- source_field: float32 [3, 256, 32, 512], P(None, 'gx', 'gy', 'gz'), may hold values from -6 to 6
- cell_contrast: bfloat16 [65536, 1536], P(('gx', 'gy', 'gz')), may hold values from 0.19921875 to 2
- point_field: bfloat16 [3, 65536], P(None, ('gx', 'gy', 'gz')), may hold values from -3 to 3
- point_class: int32 [65536, 1], P(('gx', 'gy', 'gz')), may hold values from 0 to 31; in each aligned block of 128 rows (0 to 127, 128 to 255, ...) at most 8 rows name the same one
- cell_kind: int32 [65536], P(('gx', 'gy', 'gz')), may hold values from 0 to 3
- inverse_blocks: float32 [32, 4, 3, 3, 512], P('gx'), may hold values from -0.3 to 0.3
Outputs:
- newton_step: float32 [3, 256, 32, 512], P(None, 'gx', 'gy', 'gz')
- krylov_residual: float32 [3, 256, 32, 512], P(None, 'gx', 'gy', 'gz')
The draws below stay inside these ranges and needn't reach their ends.
Inputs may be any that keep to these rules, and one draw needn't show every extreme that they name: `point_class`: among the 128 points of one device's block no class is named more than 8 times, a bound that some block reaches there.
All inputs are finite; a program needn't handle non-finite values.
Results may differ from the reference program's by a relative error of at most 0.0076.
Values may be sent and summed in bfloat16 or wider, within the bound.
A program may use at most 64 MiB of HBM per device.

```python
import math
import jax
import jax.numpy as jnp
import numpy as np
from jax import lax

CELL = 8
VOX = 512
TYPES = 4
CX = 8
CY = 8
ZP = 8
ITERS = 3
ZB = 16
Q_DEV = 128
Q_TOTAL = 65536
CLASSES = 32
CAP = 8
NX = 256
NY = 32
NZ = 512
N_GX = 32
N_GY = 4
N_GZ = 4


def plant(result, own_key, low, largest):
    extent = result.shape
    index_at = [jax.random.randint(jax.random.fold_in(own_key, axis), (), 0, extent[axis]) for axis in range(len(extent))]
    result = result.at[tuple(index_at)].set(low)
    longest = extent.index(max(extent))
    index_at[longest] = (index_at[longest] + 1) % extent[longest]
    return result.at[tuple(index_at)].set(largest)


def block_scale(stream_key, shape, shards, low, top_value):
    loudness = 1.0
    for axis_at, blocks in shards:
        draws = jax.random.uniform(jax.random.fold_in(jax.random.fold_in(stream_key, 6), axis_at), (blocks,), jnp.float32, low / len(shards), top_value / len(shards))
        loudness = loudness * jnp.repeat(jnp.exp(draws), shape[axis_at] // blocks).reshape((-1,) + (1,) * (len(shape) - 1 - axis_at))
    return loudness


def assign_block(key, own, number, rows, number_of, top, bound, skew):
    sequence = jax.random.permutation(key, number_of)
    crowded, common = portions_of(number_of, rows * top, bound, skew, True), portions_of(number_of, rows * top, bound, skew, False)
    places = jnp.arange(number_of)

    def named(sizes, turn):
        used = int((sizes > 0).sum())
        fixed = max(1, used // 4)
        moved = fixed + (places - fixed + turn * (used - fixed)) % max(1, number_of - fixed)
        return jnp.zeros((number_of,), jnp.int32).at[sequence[jnp.where(places < fixed, places, moved)]].set(jnp.asarray(sizes, jnp.int32))

    sizes = jnp.where(number % 4 == 0, named(crowded, number // 4), named(common, number - number // 4 - 1))
    mixed = jax.random.permutation(jax.random.fold_in(own, 3), number_of)
    giver, receiver = mixed[0:number_of // 2 * 2:2], mixed[1:number_of // 2 * 2:2]
    room = jnp.minimum(sizes[giver] - 1, bound - sizes[receiver]) // 2
    room = jnp.where((giver == sequence[0]) | (receiver == sequence[0]) | (sizes[receiver] == 0), 0, jnp.maximum(room, 0))
    moved = jax.random.randint(jax.random.fold_in(own, 4), (number_of // 2,), 0, 1 << 20) % (room + 1)
    sizes = sizes.at[giver].add(-moved).at[receiver].add(moved)
    labels = jnp.searchsorted(jnp.cumsum(sizes), jnp.arange(rows * top), side="right").astype(jnp.int32)
    grid = labels.reshape(top, rows).T
    grid = grid[jax.random.permutation(jax.random.fold_in(own, 1), rows)]
    turn = jax.random.randint(jax.random.fold_in(own, 2), (rows, 1), 0, top)
    return jnp.take_along_axis(grid, (jnp.arange(top)[None, :] + turn) % top, axis=1)


def portions_of(amount, total, limit, lean, full):
    loads = [(1 << 20) // math.isqrt(rank ** lean) + 1 for rank in range(1, amount + 1)]
    largest = limit if full else min(limit, max(-(-total // amount), total * loads[0] // sum(loads)))
    least = 1 if total - largest >= amount - 1 else 0
    holding, spare = [largest] + [least] * (amount - 1), total - largest - least * (amount - 1)
    while spare > 0:
        movable = [i for i in range(1, amount) if holding[i] < largest] or [i for i in range(1, amount) if holding[i] < limit]
        mass, remaining = sum([loads[i] for i in movable]), spare
        for i in movable:
            extra = min(limit - holding[i], max(1, remaining * loads[i] // mass), spare)
            holding[i] = holding[i] + extra
            spare = spare - extra
    return np.array(holding)


def gaussian(key, dims, width, reach, pieces=(), kind=jnp.bfloat16):
    gain = block_scale(key, dims, pieces, -0.22, 0.18) if pieces else 1.0
    entries = jax.random.normal(key, dims, jnp.float32) * width * gain
    return jnp.minimum(jnp.maximum(entries, -reach), reach).astype(kind)


def setup_inputs(seed: int = 0) -> dict:
    key_of = jax.random.split(jax.random.key(seed), 7)
    source_field = gaussian(key_of[0], (3, NX, NY, NZ), 1.0, 6.0, ((1, 32), (2, 4), (3, 4)), jnp.float32)
    cell_contrast = jnp.clip(jnp.exp(math.log(2.0) - 2.306499 * jax.random.uniform(key_of[1], (Q_TOTAL, 3 * VOX), jnp.float32) ** block_scale(key_of[1], (Q_TOTAL, 3 * VOX), ((0, 512),), -0.2, 0.2)), 0.19921875, 2.0).astype(jnp.bfloat16)
    point_field = gaussian(key_of[2], (3, Q_TOTAL), 1.0, 3.0, ((1, 512),))
    point_class_keys = jax.random.split(jax.random.fold_in(key_of[3], 1), Q_TOTAL // Q_DEV)
    point_class_turns = jax.random.permutation(jax.random.fold_in(key_of[3], 3), Q_TOTAL // Q_DEV)
    point_class = jax.vmap(lambda own, number: assign_block(jax.random.fold_in(key_of[3], 2), own, number, Q_DEV, CLASSES, 1, CAP, 2))(point_class_keys, point_class_turns).reshape((Q_TOTAL, 1))
    cell_kind = plant(jax.random.randint(key_of[4], (Q_TOTAL,), 0, TYPES), jax.random.fold_in(key_of[4], 1), 0, TYPES - 1).astype(jnp.int32)
    inverse_blocks = jnp.clip(jax.random.uniform(key_of[5], (CLASSES, TYPES, 3, 3, VOX), jnp.float32, -0.3, 0.3) * block_scale(key_of[5], (CLASSES, TYPES, 3, 3, VOX), ((0, 32),), -0.4, 0.0), -0.3, 0.3)
    return {"source_field": source_field, "cell_contrast": cell_contrast, "point_field": point_field, "point_class": point_class, "cell_kind": cell_kind, "inverse_blocks": inverse_blocks}


kerr_scale = 0.1

def hartley_table():
    voxel_index = jnp.arange(VOX, dtype=jnp.int32)
    along_one = voxel_index // (CELL * CELL)
    along_two = voxel_index // CELL % CELL
    along_three = voxel_index % CELL
    phase_index = (along_one[:, None] * along_one[None, :] + along_two[:, None] * along_two[None, :] + along_three[:, None] * along_three[None, :]) % CELL
    phase_angle = 2.0 * math.pi / CELL * phase_index.astype(jnp.float32)
    return ((jnp.cos(phase_angle) + jnp.sin(phase_angle)) / math.sqrt(VOX)).astype(jnp.bfloat16)

def cell_solve(contrast, point_values, blocks, hartley):
    row_count = contrast.shape[0]
    weights = contrast.reshape(row_count, 3, VOX).astype(jnp.float32)
    base_field = point_values.astype(jnp.float32)[:, :, None]

    def correction(polarization):
        spectrum = jnp.dot(polarization.reshape(row_count * 3, VOX), hartley, preferred_element_type=jnp.float32).reshape(row_count, 3, VOX)
        mixed_spectrum = lax.optimization_barrier(jnp.sum(blocks * spectrum[:, None, :, :], axis=2)).astype(jnp.bfloat16)
        return jnp.dot(mixed_spectrum.reshape(row_count * 3, VOX), hartley, preferred_element_type=jnp.float32).reshape(row_count, 3, VOX)
    local_field = base_field - correction((weights * base_field).astype(jnp.bfloat16))
    kerr_polar = (weights * local_field * (1.0 + kerr_scale * local_field * local_field)).astype(jnp.bfloat16)
    final_field = base_field - correction(kerr_polar)
    flux_mean = lax.optimization_barrier(jnp.mean((1.0 + weights) * final_field, axis=2))
    stiffness = 0.5 + lax.optimization_barrier(jnp.mean(weights * final_field * final_field, axis=(1, 2)))
    return jnp.concatenate([flux_mean, stiffness[:, None]], axis=1)

def to_grid(point_rows):
    comps = point_rows.shape[0]
    shaped = point_rows.reshape(comps, N_GX, N_GY, N_GZ, CY, ZB).transpose(0, 1, 2, 4, 3, 5)
    shaped = shaped.reshape(comps, N_GX, 1, N_GY, CY, N_GZ, ZB, 1)
    return jnp.broadcast_to(shaped, (comps, N_GX, CX, N_GY, CY, N_GZ, ZB, ZP)).reshape(comps, NX, NY, NZ)

def operate(field, diagonal):
    padded = jnp.pad(field, ((0, 0), (1, 1), (1, 1), (1, 1)))
    beside = padded[:, 2:, 1:-1, 1:-1] + padded[:, :-2, 1:-1, 1:-1]
    beside = beside + padded[:, 1:-1, 2:, 1:-1] + padded[:, 1:-1, :-2, 1:-1]
    beside = beside + padded[:, 1:-1, 1:-1, 2:] + padded[:, 1:-1, 1:-1, :-2]
    return (6.0 + diagonal)[None] * field - beside

def reference(source_field, cell_contrast, point_field, point_class, cell_kind, inverse_blocks):
    hartley = hartley_table()
    point_total = cell_contrast.shape[0]
    block_size = math.gcd(point_total, 256)
    block_count = point_total // block_size

    def one_block(packed):
        contrast, point_values, classes, kinds = packed
        blocks = inverse_blocks[classes, kinds]
        return cell_solve(contrast, point_values, blocks, hartley)
    results = lax.map(one_block, (cell_contrast.reshape(block_count, block_size, 3 * VOX), point_field.T.reshape(block_count, block_size, 3), point_class[:, 0].reshape(block_count, block_size), cell_kind.reshape(block_count, block_size)))
    summary = results.reshape(point_total, 4)
    stiffness_grid = to_grid(summary[:, 3][None, :])[0]
    flux_grid = to_grid(summary[:, :3].T)
    right = source_field - flux_grid
    newton_step = jnp.zeros_like(right)
    residual, direction = (right, right)
    norm_now = jnp.sum(residual * residual)
    for iteration in range(ITERS):
        image = operate(direction, stiffness_grid)
        alpha = norm_now / jnp.sum(direction * image)
        newton_step = newton_step + alpha * direction
        residual = residual - alpha * image
        norm_next = jnp.sum(residual * residual)
        direction = residual + norm_next / norm_now * direction
        norm_now = norm_next
    return (newton_step, residual)
```

```python
import functools
import math

import jax
import jax.numpy as jnp
import numpy as np
from jax import lax
from jax.experimental import pallas as pl
from jax.experimental.pallas import tpu as pltpu
from jax.sharding import PartitionSpec as P

CELL = 8
VOX = 512
TYPES = 4
ZP = 8
ITERS = 3
NGX = 32
NZC = 16
NP = 16
PART = 128
ROW = 9 * PART
SLAB = ROW + PART
POINTS = 128
FIELDS = 24
KERR = 0.1
SHIFT = 7.0
THETA = 2.0**-12

MESH = pl.DeviceIdType.MESH
F32 = jnp.float32
BF16 = jnp.bfloat16


def hartley_table():
    n = np.arange(VOX)
    a, b, c = n // (CELL * CELL), n // CELL % CELL, n % CELL
    phase = (np.outer(a, a) + np.outer(b, b) + np.outer(c, c)) % CELL
    angle = 2.0 * math.pi / CELL * np.arange(CELL)
    values = ((np.cos(angle) + np.sin(angle)) / math.sqrt(VOX)).astype(np.float32)
    values[np.abs(values) < 1e-6] = 0.0
    return values.astype(jnp.bfloat16)[phase]


def kernel(
    source_ref,
    contrast_ref,
    point_ref,
    class_ref,
    kind_ref,
    inverse_ref,
    hartley_ref,
    step_ref,
    residual_ref,
    slice_buf,
    column_buf,
    lib,
    blocks,
    basis,
    out_x,
    out_y,
    out_z,
    in_x,
    in_y,
    in_z,
    plane_buf,
    line_buf,
    send_one,
    recv_one,
    send_two,
    recv_two,
    send_three,
    recv_three,
    send_halo,
    recv_halo,
    send_plane,
    recv_plane,
    send_line,
    recv_line,
):
    gx, gy, gz = lax.axis_index("gx"), lax.axis_index("gy"), lax.axis_index("gz")
    chip, core = gx // 2, gx % 2
    place = gy * 4 + gz

    def on_line(target):
        return {"gx": target, "gy": gy, "gz": gz}

    def on_plane(target):
        return {"gx": gx, "gy": target // 4, "gz": target % 4}

    barrier = pltpu.get_barrier_semaphore()

    @pl.loop(1, NGX)
    def _(d):
        pl.semaphore_signal(
            barrier, inc=1, device_id=on_line(lax.rem(gx + d, NGX)), device_id_type=MESH
        )

    @pl.loop(1, NP)
    def _(d):
        pl.semaphore_signal(
            barrier, inc=1, device_id=on_plane(lax.rem(place + d, NP)), device_id_type=MESH
        )

    for i in range(3):
        for j in range(3):
            at = (i * 3 + j) * PART
            slice_buf[:, at : at + PART] = inverse_ref[
                0, gy, i, j : j + 1, pl.ds(pl.multiple_of(gz * PART, PART), PART)
            ]
    column_buf[chip] = slice_buf[...]
    pl.semaphore_wait(barrier, NGX - 1 + NP - 1)

    def one(d):
        to = lax.rem(chip + d, NZC)
        return pltpu.make_async_remote_copy(
            src_ref=slice_buf,
            dst_ref=column_buf.at[chip],
            send_sem=send_one.at[d],
            recv_sem=recv_one.at[chip],
            device_id=on_line(to * 2 + core),
            device_id_type=MESH,
        )

    def one_arrival(d):
        source = lax.rem(chip + NZC - d, NZC)
        return pltpu.make_async_remote_copy(
            src_ref=slice_buf,
            dst_ref=column_buf.at[source],
            send_sem=send_one.at[d],
            recv_sem=recv_one.at[source],
            device_id=on_line(source * 2 + core),
            device_id_type=MESH,
        )

    @pl.loop(1, NZC)
    def _(d):
        one(d).start()

    rows = lax.broadcasted_iota(jnp.int32, (8, POINTS), 0)
    point = point_ref[...].astype(F32)
    packed = jnp.zeros((8, POINTS), F32)
    for i in range(3):
        packed = jnp.where(rows == i, jnp.broadcast_to(point[i : i + 1], (8, POINTS)), packed)
    packed = jnp.where(
        rows == 3, jnp.broadcast_to(kind_ref[...].astype(F32), (8, POINTS)), packed
    )
    columns = packed.T
    base = [columns[:, i : i + 1] for i in range(3)]
    kind = columns[:, 3:4].astype(jnp.int32)
    owner = class_ref[...]
    key = kind * NGX + (owner % 2) * NZC + owner // 2
    hot = (lax.broadcasted_iota(jnp.int32, (POINTS, POINTS), 1) == key).astype(F32).astype(BF16)
    weights = [contrast_ref[:, i * VOX : (i + 1) * VOX].astype(F32) for i in range(3)]

    def spectrum_of(polar):
        return [
            jnp.dot(polar[i], hartley_ref[...], preferred_element_type=F32) for i in range(3)
        ]

    first = spectrum_of([(weights[i] * base[i]).astype(BF16) for i in range(3)])

    @pl.loop(1, NZC)
    def _(d):
        one_arrival(d).wait_recv()

    mine = (gz * 4 + gy) * 2 + core
    wide = column_buf[...].reshape(NZC, ROW)
    narrow = wide.astype(BF16)
    lib[mine, :, 0:ROW] = narrow
    rest = wide - narrow.astype(F32)
    lanes = lax.broadcasted_iota(jnp.int32, (NZC, PART), 1)
    tail = jnp.zeros((NZC, PART), F32)
    for n in range(9):
        lead = jnp.broadcast_to(rest[:, n * PART : n * PART + 1], (NZC, PART))
        tail = jnp.where(lanes == n, lead, tail)
    lib[mine, :, ROW:SLAB] = tail.astype(BF16)

    def two(d):
        return pltpu.make_async_remote_copy(
            src_ref=lib.at[mine],
            dst_ref=lib.at[mine],
            send_sem=send_two.at[d],
            recv_sem=recv_two.at[place],
            device_id=on_plane(lax.rem(place + d, NP)),
            device_id_type=MESH,
        )

    def slab_of(where):
        return (where % 4 * 4 + where // 4) * 2

    def two_arrival(d):
        source = lax.rem(place + NP - d, NP)
        at = slab_of(source) + core
        return pltpu.make_async_remote_copy(
            src_ref=lib.at[at],
            dst_ref=lib.at[at],
            send_sem=send_two.at[d],
            recv_sem=recv_two.at[source],
            device_id=on_plane(source),
            device_id_type=MESH,
        )

    def three(where, which):
        at = slab_of(where) + which
        return pltpu.make_async_remote_copy(
            src_ref=lib.at[at],
            dst_ref=lib.at[at],
            send_sem=send_three.at[where],
            recv_sem=recv_three.at[where],
            device_id=on_line(chip * 2 + 1 - core),
            device_id_type=MESH,
        )

    @pl.loop(1, NP)
    def _(d):
        two(d).start()

    three(place, core).start()

    @pl.loop(1, NP)
    def _(d):
        two_arrival(d).wait_recv()
        three(lax.rem(place + NP - d, NP), core).start()

    @pl.loop(0, NP)
    def _(w):
        three(w, 1 - core).wait_recv()

    for f in range(4):
        part = lib[f * 8 : (f + 1) * 8].reshape(POINTS, SLAB)
        chosen = jnp.dot(hot, part, preferred_element_type=F32)
        if f:
            blocks[f] = chosen[:, 0:ROW]
        else:
            lead = lax.broadcasted_iota(jnp.int32, (POINTS, PART), 1) == 0
            for n in range(9):
                tail = jnp.broadcast_to(chosen[:, ROW + n : ROW + n + 1], (POINTS, PART))
                blocks[f, :, n * PART : (n + 1) * PART] = chosen[
                    :, n * PART : (n + 1) * PART
                ] + jnp.where(lead, tail, 0.0)

    def correction(spectrum):
        mixed = []
        for i in range(3):
            parts = []
            for f in range(4):
                total = None
                for j in range(3):
                    at = (i * 3 + j) * PART
                    term = (
                        blocks[f, :, at : at + PART]
                        * spectrum[j][:, f * PART : (f + 1) * PART]
                    )
                    total = term if total is None else total + term
                parts.append(total.astype(BF16))
            mixed.append(jnp.concatenate(parts, axis=1))
        return spectrum_of(mixed)

    local = [base[i] - c for i, c in enumerate(correction(first))]
    polar = [
        (weights[i] * local[i] * (1.0 + KERR * local[i] * local[i])).astype(BF16)
        for i in range(3)
    ]
    final = [base[i] - c for i, c in enumerate(correction(spectrum_of(polar)))]
    flux = [
        jnp.sum((1.0 + weights[i]) * final[i], axis=1, keepdims=True) * (1.0 / VOX)
        for i in range(3)
    ]
    energy = sum(weights[i] * final[i] * final[i] for i in range(3))
    stiff = 0.5 + jnp.sum(energy, axis=1, keepdims=True) * (1.0 / (3 * VOX))

    q = lax.broadcasted_iota(jnp.int32, (POINTS, PART), 0)
    z = lax.broadcasted_iota(jnp.int32, (POINTS, PART), 1)
    here = (q % 16) == (z // ZP)

    def to_plane(column):
        spread = jnp.where(here, jnp.broadcast_to(column, (POINTS, PART)), 0.0)
        return jnp.sum(spread.reshape(8, 16, PART), axis=1)

    diagonal = (to_plane(stiff) + (6.0 - SHIFT)) * THETA
    for c in range(3):
        plane = to_plane(flux[c])
        for x in range(8):
            basis[0, (c * 8 + x) * 8 : (c * 8 + x + 1) * 8, :] = source_ref[c, x] - plane

    lane = lax.broadcasted_iota(jnp.int32, (8, PART), 1)
    sub = lax.broadcasted_iota(jnp.int32, (8, PART), 0)
    sides = (
        on_line(lax.rem(gx + NGX - 1, NGX)),
        on_line(lax.rem(gx + 1, NGX)),
        {"gx": gx, "gy": lax.rem(gy + 3, 4), "gz": gz},
        {"gx": gx, "gy": lax.rem(gy + 1, 4), "gz": gz},
        {"gx": gx, "gy": gy, "gz": lax.rem(gz + 3, 4)},
        {"gx": gx, "gy": gy, "gz": lax.rem(gz + 1, 4)},
    )
    out_bufs = (out_x, out_x, out_y, out_y, out_z, out_z)
    in_bufs = (in_x, in_x, in_y, in_y, in_z, in_z)

    def halo(step, side):
        low = side % 2
        return pltpu.make_async_remote_copy(
            src_ref=out_bufs[side].at[step, low],
            dst_ref=in_bufs[side].at[step, 1 - low],
            send_sem=send_halo.at[step, side],
            recv_sem=recv_halo.at[step, side - low + 1 - low],
            device_id=sides[side],
            device_id_type=MESH,
        )

    def halo_arrival(step, side):
        low = side % 2
        return pltpu.make_async_remote_copy(
            src_ref=out_bufs[side].at[step, low],
            dst_ref=in_bufs[side].at[step, low],
            send_sem=send_halo.at[step, side],
            recv_sem=recv_halo.at[step, side],
            device_id=sides[side],
            device_id_type=MESH,
        )

    def tile(level, n):
        return basis[level, n * 8 : (n + 1) * 8, :]

    def dot(a, b):
        total = tile(a, 0) * tile(b, 0)
        for n in range(1, FIELDS):
            total = total + tile(a, n) * tile(b, n)
        return jnp.sum(total, axis=0, keepdims=True)

    first_x, last_x = gx == 0, gx == NGX - 1
    first_y, last_y = gy == 0, gy == 3
    first_z, last_z = gz == 0, gz == 3
    moments = []

    for step in range(ITERS):
        low_z = jnp.zeros((8, PART), F32)
        high_z = jnp.zeros((8, PART), F32)
        for c in range(3):
            out_x[step, 0, c * 8 : (c + 1) * 8, :] = tile(step, c * 8)
            out_x[step, 1, c * 8 : (c + 1) * 8, :] = tile(step, c * 8 + 7)
        halo(step, 0).start()
        halo(step, 1).start()
        out_y[step, 0] = basis[step, pl.ds(0, FIELDS, stride=8), :]
        out_y[step, 1] = basis[step, pl.ds(7, FIELDS, stride=8), :]
        halo(step, 2).start()
        halo(step, 3).start()
        for n in range(FIELDS):
            value = tile(step, n)
            low_z = jnp.where(lane == n, pltpu.roll(value, n, 1), low_z)
            high_z = jnp.where(lane == n, pltpu.roll(value, n + 1, 1), high_z)
        out_z[step, 0] = low_z
        out_z[step, 1] = high_z
        halo(step, 4).start()
        halo(step, 5).start()
        if step:
            moments.append(dot(step - 1, step))
        moments.append(dot(step, step))
        for side in range(6):
            halo_arrival(step, side).wait_recv()
        from_low = jnp.where(first_z, 0.0, in_z[step, 0])
        from_high = jnp.where(last_z, 0.0, in_z[step, 1])
        rows_low = jnp.where(first_y, 0.0, in_y[step, 0])
        rows_high = jnp.where(last_y, 0.0, in_y[step, 1])
        for c in range(3):
            edge_low = jnp.where(first_x, 0.0, in_x[step, 0, c * 8 : (c + 1) * 8, :])
            edge_high = jnp.where(last_x, 0.0, in_x[step, 1, c * 8 : (c + 1) * 8, :])
            for x in range(8):
                n = c * 8 + x
                value = tile(step, n)
                beside = edge_low if x == 0 else tile(step, n - 1)
                beside = beside + (edge_high if x == 7 else tile(step, n + 1))
                row_low = jnp.broadcast_to(rows_low[n : n + 1], (8, PART))
                row_high = jnp.broadcast_to(rows_high[n : n + 1], (8, PART))
                beside = beside + jnp.where(sub == 0, row_low, pltpu.roll(value, 1, 0))
                beside = beside + jnp.where(sub == 7, row_high, pltpu.roll(value, 7, 0))
                side_low = jnp.broadcast_to(from_low[:, n : n + 1], (8, PART))
                side_high = jnp.broadcast_to(from_high[:, n : n + 1], (8, PART))
                beside = beside + jnp.where(lane == 0, side_low, pltpu.roll(value, 1, 1))
                beside = beside + jnp.where(
                    lane == PART - 1, side_high, pltpu.roll(value, PART - 1, 1)
                )
                basis[step + 1, n * 8 : (n + 1) * 8, :] = diagonal * value - THETA * beside
    moments.append(dot(ITERS - 1, ITERS))

    stacked = jnp.zeros((8, PART), F32)
    for k, moment in enumerate(moments):
        stacked = jnp.where(sub == k, jnp.broadcast_to(moment, (8, PART)), stacked)
    plane_buf[place] = stacked

    def plane_copy(d):
        return pltpu.make_async_remote_copy(
            src_ref=plane_buf.at[place],
            dst_ref=plane_buf.at[place],
            send_sem=send_plane.at[d],
            recv_sem=recv_plane.at[place],
            device_id=on_plane(lax.rem(place + d, NP)),
            device_id_type=MESH,
        )

    def plane_arrival(d):
        source = lax.rem(place + NP - d, NP)
        return pltpu.make_async_remote_copy(
            src_ref=plane_buf.at[source],
            dst_ref=plane_buf.at[source],
            send_sem=send_plane.at[d],
            recv_sem=recv_plane.at[source],
            device_id=on_plane(source),
            device_id_type=MESH,
        )

    def line_copy(d):
        return pltpu.make_async_remote_copy(
            src_ref=line_buf.at[gx],
            dst_ref=line_buf.at[gx],
            send_sem=send_line.at[d],
            recv_sem=recv_line.at[gx],
            device_id=on_line(lax.rem(gx + d, NGX)),
            device_id_type=MESH,
        )

    def line_arrival(d):
        source = lax.rem(gx + NGX - d, NGX)
        return pltpu.make_async_remote_copy(
            src_ref=line_buf.at[source],
            dst_ref=line_buf.at[source],
            send_sem=send_line.at[d],
            recv_sem=recv_line.at[source],
            device_id=on_line(source),
            device_id_type=MESH,
        )

    @pl.loop(1, NP)
    def _(d):
        plane_copy(d).start()

    @pl.loop(1, NP)
    def _(d):
        plane_arrival(d).wait_recv()

    line_buf[gx] = jnp.sum(plane_buf[...], axis=0)

    @pl.loop(1, NGX)
    def _(d):
        line_copy(d).start()

    @pl.loop(1, NGX)
    def _(d):
        line_arrival(d).wait_recv()

    total = jnp.sum(jnp.sum(line_buf[...], axis=0), axis=1, keepdims=True)
    m = [total[k : k + 1] for k in range(6)]

    def product(a, b):
        result = None
        for i, left in enumerate(a):
            for j, right in enumerate(b):
                term = left * (right * m[i + j])
                result = term if result is None else result + term
        return result

    unit = jnp.ones((1, 1), F32)
    now = [unit]
    course = [unit]
    taken = []
    norm = m[0]
    for step in range(ITERS):
        image = [SHIFT * course[0]]
        for k in range(1, len(course)):
            image.append(SHIFT * course[k] + (1.0 / THETA) * course[k - 1])
        image.append((1.0 / THETA) * course[-1])
        alpha = norm / product(course, image)
        taken = [
            alpha * g + (taken[k] if k < len(taken) else 0.0) for k, g in enumerate(course)
        ]
        now = [
            (now[k] if k < len(now) else 0.0) - alpha * g for k, g in enumerate(image)
        ]
        if step < ITERS - 1:
            following = product(now, now)
            beta = following / norm
            course = [
                g + (beta * course[k] if k < len(course) else 0.0) for k, g in enumerate(now)
            ]
            norm = following
    taken = [jnp.broadcast_to(g, (8, PART)) for g in taken]
    now = [jnp.broadcast_to(g, (8, PART)) for g in now]
    for n in range(FIELDS):
        values = [tile(k, n) for k in range(ITERS + 1)]
        step_ref[n // 8, n % 8] = sum(taken[k] * values[k] for k in range(ITERS))
        residual_ref[n // 8, n % 8] = sum(now[k] * values[k] for k in range(ITERS + 1))

    @pl.loop(1, NZC)
    def _(d):
        one(d).wait_send()

    @pl.loop(1, NP)
    def _(d):
        two(d).wait_send()
        plane_copy(d).wait_send()

    @pl.loop(0, NP)
    def _(w):
        three(w, core).wait_send()

    for step in range(ITERS):
        for side in range(6):
            halo(step, side).wait_send()

    @pl.loop(1, NGX)
    def _(d):
        line_copy(d).wait_send()


def per_device(source_field, cell_contrast, point_field, point_class, cell_kind, inverse_blocks):
    vmem = pl.BlockSpec(memory_space=pltpu.VMEM)
    dma = pltpu.SemaphoreType.DMA
    shape = jax.ShapeDtypeStruct(source_field.shape, F32)
    return pl.pallas_call(
        kernel,
        out_shape=(shape, shape),
        in_specs=[vmem] * 7,
        out_specs=(vmem, vmem),
        scratch_shapes=[
            pltpu.VMEM((1, ROW), F32),
            pltpu.VMEM((NZC, 1, ROW), F32),
            pltpu.VMEM((2 * NP, NZC, SLAB), BF16),
            pltpu.VMEM((4, POINTS, ROW), F32),
            pltpu.VMEM((ITERS + 1, FIELDS * 8, PART), F32),
            pltpu.VMEM((ITERS, 2, FIELDS, PART), F32),
            pltpu.VMEM((ITERS, 2, FIELDS, PART), F32),
            pltpu.VMEM((ITERS, 2, 8, PART), F32),
            pltpu.VMEM((ITERS, 2, FIELDS, PART), F32),
            pltpu.VMEM((ITERS, 2, FIELDS, PART), F32),
            pltpu.VMEM((ITERS, 2, 8, PART), F32),
            pltpu.VMEM((NP, 8, PART), F32),
            pltpu.VMEM((NGX, 8, PART), F32),
            dma((NZC,)),
            dma((NZC,)),
            dma((NP,)),
            dma((NP,)),
            dma((NP,)),
            dma((NP,)),
            dma((ITERS, 6)),
            dma((ITERS, 6)),
            dma((NP,)),
            dma((NP,)),
            dma((NGX,)),
            dma((NGX,)),
        ],
        compiler_params=pltpu.CompilerParams(
            collective_id=0, has_side_effects=True, vmem_limit_bytes=40 << 20
        ),
    )(
        source_field,
        cell_contrast,
        point_field,
        point_class,
        cell_kind.reshape(1, -1),
        inverse_blocks,
        jnp.asarray(hartley_table()),
    )


def solution(mesh):
    placed = (
        P(None, "gx", "gy", "gz"),
        P(("gx", "gy", "gz"), None),
        P(None, ("gx", "gy", "gz")),
        P(("gx", "gy", "gz"), None),
        P(("gx", "gy", "gz")),
        P("gx", None, None, None, None),
    )
    return jax.shard_map(
        per_device,
        mesh=mesh,
        in_specs=placed,
        out_specs=(P(None, "gx", "gy", "gz"), P(None, "gx", "gy", "gz")),
        check_vma=False,
    )
```

```python
import functools
import math

import jax
import jax.numpy as jnp
import numpy as np
from jax import lax
from jax.experimental import pallas as pl
from jax.experimental.pallas import tpu as pltpu
from jax.sharding import PartitionSpec as P

CELL = 8
VOX = 512
TYPES = 4
ZP = 8
ITERS = 3
NGX = 32
NZC = 16
NP = 16
OWN = 3
PART = 128
ROW = 9 * PART
SLAB = ROW + PART
POINTS = 128
FIELDS = 24
KERR = 0.1
SHIFT = 7.0
THETA = 2.0**-12

MESH = pl.DeviceIdType.MESH
F32 = jnp.float32
BF16 = jnp.bfloat16


def hartley_table():
    n = np.arange(VOX)
    a, b, c = n // (CELL * CELL), n // CELL % CELL, n % CELL
    phase = (np.outer(a, a) + np.outer(b, b) + np.outer(c, c)) % CELL
    angle = 2.0 * math.pi / CELL * np.arange(CELL)
    values = ((np.cos(angle) + np.sin(angle)) / math.sqrt(VOX)).astype(np.float32)
    values[np.abs(values) < 1e-6] = 0.0
    return values.astype(jnp.bfloat16)[phase]


def kernel(
    source_hbm,
    contrast_hbm,
    point_hbm,
    class_hbm,
    kind_hbm,
    inverse_hbm,
    hartley_hbm,
    level_0,
    level_1,
    level_2,
    level_3,
    weight_0,
    weight_1,
    weight_2,
    weight_3,
    weight_4,
    weight_5,
    weight_6,
    source_ref,
    contrast_ref,
    point_ref,
    class_ref,
    kind_ref,
    inverse_ref,
    hartley_ref,
    slice_buf,
    column_buf,
    lib,
    blocks,
    out_halo,
    in_halo,
    plane_buf,
    line_buf,
    load_sems,
    send_one,
    recv_one,
    send_two,
    recv_two,
    send_three,
    recv_three,
    send_halo,
    recv_halo,
    send_sum,
    recv_sum,
):
    gx, gy, gz = lax.axis_index("gx"), lax.axis_index("gy"), lax.axis_index("gz")
    chip, core = gx // 2, gx % 2
    place = gy * 4 + gz
    basis = (level_0, level_1, level_2, level_3)
    weights_out = (weight_0, weight_1, weight_2, weight_3, weight_4, weight_5, weight_6)

    def on_line(target):
        return {"gx": target, "gy": gy, "gz": gz}

    def on_plane(target):
        return {"gx": gx, "gy": target // 4, "gz": target % 4}

    barrier = pltpu.get_barrier_semaphore()
    for d in sorted(range(1, NGX), key=lambda d: -min(d, NGX - d)):
        pl.semaphore_signal(
            barrier, inc=1, device_id=on_line(lax.rem(gx + d, NGX)), device_id_type=MESH
        )
    for d in range(1, NP):
        pl.semaphore_signal(
            barrier, inc=1, device_id=on_plane(lax.rem(place + d, NP)), device_id_type=MESH
        )

    loads = [
        pltpu.make_async_copy(
            inverse_hbm.at[:, :, pl.ds(pl.multiple_of(gz * PART, PART), PART)],
            inverse_ref,
            load_sems.at[0],
        )
    ]
    pairs = (
        (point_hbm, point_ref),
        (class_hbm, class_ref),
        (kind_hbm, kind_ref),
        (contrast_hbm, contrast_ref),
        (hartley_hbm, hartley_ref),
        (source_hbm, source_ref),
    )
    for n, (origin, goal) in enumerate(pairs):
        loads.append(pltpu.make_async_copy(origin, goal, load_sems.at[n + 1]))
    for load in loads:
        load.start()
    loads[0].wait()

    for n in range(9):
        slice_buf[:, n * PART : (n + 1) * PART] = inverse_ref[n, pl.ds(gy, 1), :]
    column_buf[OWN] = slice_buf[...]

    for load in loads[1:]:
        load.wait()
    rows = lax.broadcasted_iota(jnp.int32, (8, POINTS), 0)
    point = point_ref[...].astype(F32)
    packed = jnp.zeros((8, POINTS), F32)
    entries = [point[i : i + 1] for i in range(3)]
    entries += [kind_ref[...].astype(F32), class_ref[...].astype(F32)]
    for i, entry in enumerate(entries):
        packed = jnp.where(rows == i, jnp.broadcast_to(entry, (8, POINTS)), packed)
    columns = packed.T
    base = [columns[:, i : i + 1] for i in range(3)]
    kind = columns[:, 3:4].astype(jnp.int32)
    owner = columns[:, 4:5].astype(jnp.int32)
    away = (owner // 2 - chip + OWN + NZC) % NZC
    key = (away // 8) * 64 + (owner % 2) * 32 + kind * 8 + away % 8
    hot = (lax.broadcasted_iota(jnp.int32, (POINTS, POINTS), 1) == key).astype(F32).astype(BF16)
    weights = [contrast_ref[:, i * VOX : (i + 1) * VOX].astype(F32) for i in range(3)]

    def spectrum_of(polar):
        return [
            jnp.dot(polar[i], hartley_ref[...], preferred_element_type=F32) for i in range(3)
        ]

    first = spectrum_of([(weights[i] * base[i]).astype(BF16) for i in range(3)])

    pl.semaphore_wait(barrier, NGX - 1 + NP - 1)

    def one(d):
        slot = (OWN - d) % NZC
        return pltpu.make_async_remote_copy(
            src_ref=slice_buf,
            dst_ref=column_buf.at[slot],
            send_sem=send_one,
            recv_sem=recv_one.at[slot // 8],
            device_id=on_line(lax.rem(chip + d, NZC) * 2 + core),
            device_id_type=MESH,
        )

    for d in sorted(range(1, NZC), key=lambda d: -min(d, NZC - d)):
        one(d).start()

    def drain(region, send_sem, recv_sem):
        return pltpu.make_async_remote_copy(
            src_ref=region,
            dst_ref=region,
            send_sem=send_sem,
            recv_sem=recv_sem,
            device_id=on_line(chip * 2 + 1 - core),
            device_id_type=MESH,
        )

    def two(half, d):
        at = lib.at[half, core, place]
        return pltpu.make_async_remote_copy(
            src_ref=at,
            dst_ref=at,
            send_sem=send_two.at[half],
            recv_sem=recv_two.at[half],
            device_id=on_plane(lax.rem(place + d, NP)),
            device_id_type=MESH,
        )

    def three(half, which):
        return drain(lib.at[half, which], send_three.at[half], recv_three.at[half])

    lanes = lax.broadcasted_iota(jnp.int32, (8, PART), 1)
    for half in range(2):
        count = 7 if half == 0 else 8
        drain(column_buf.at[pl.ds(half * 8, count)], send_one, recv_one.at[half]).wait_recv()
        wide = column_buf[half * 8 : (half + 1) * 8].reshape(8, ROW)
        narrow = wide.astype(BF16)
        lib[half, core, place, :, 0:ROW] = narrow
        rest = wide - narrow.astype(F32)
        tail = jnp.zeros((8, PART), F32)
        for n in range(9):
            lead = jnp.broadcast_to(rest[:, n * PART : n * PART + 1], (8, PART))
            tail = jnp.where(lanes == n, lead, tail)
        lib[half, core, place, :, ROW:SLAB] = tail.astype(BF16)
        for d in range(1, NP):
            two(half, d).start()

    for half in range(2):
        region = lib.at[half, core, pl.ds(0, NP - 1)]
        drain(region, send_two.at[half], recv_two.at[half]).wait_recv()
        three(half, core).start()
    for half in range(2):
        three(half, 1 - core).wait_recv()

    for f in range(4):
        part = jnp.concatenate(
            [lib[half, c, k * 4 + f] for half in range(2) for c in range(2) for k in range(4)],
            axis=0,
        )
        chosen = jnp.dot(hot, part, preferred_element_type=F32)
        if f:
            blocks[f] = chosen[:, 0:ROW]
        else:
            lead = lax.broadcasted_iota(jnp.int32, (POINTS, PART), 1) == 0
            for n in range(9):
                tail = jnp.broadcast_to(chosen[:, ROW + n : ROW + n + 1], (POINTS, PART))
                blocks[f, :, n * PART : (n + 1) * PART] = chosen[
                    :, n * PART : (n + 1) * PART
                ] + jnp.where(lead, tail, 0.0)

    def correction(spectrum):
        mixed = []
        for i in range(3):
            parts = []
            for f in range(4):
                total = None
                for j in range(3):
                    at = (i * 3 + j) * PART
                    term = (
                        blocks[f, :, at : at + PART]
                        * spectrum[j][:, f * PART : (f + 1) * PART]
                    )
                    total = term if total is None else total + term
                parts.append(total.astype(BF16))
            mixed.append(jnp.concatenate(parts, axis=1))
        return spectrum_of(mixed)

    local = [base[i] - c for i, c in enumerate(correction(first))]
    polar = [
        (weights[i] * local[i] * (1.0 + KERR * local[i] * local[i])).astype(BF16)
        for i in range(3)
    ]
    final = [base[i] - c for i, c in enumerate(correction(spectrum_of(polar)))]
    flux = [
        jnp.sum((1.0 + weights[i]) * final[i], axis=1, keepdims=True) * (1.0 / VOX)
        for i in range(3)
    ]
    energy = sum(weights[i] * final[i] * final[i] for i in range(3))
    stiff = 0.5 + jnp.sum(energy, axis=1, keepdims=True) * (1.0 / (3 * VOX))

    q = lax.broadcasted_iota(jnp.int32, (POINTS, PART), 0)
    z = lax.broadcasted_iota(jnp.int32, (POINTS, PART), 1)
    here = (q % 16) == (z // ZP)

    def to_plane(column):
        spread = jnp.where(here, jnp.broadcast_to(column, (POINTS, PART)), 0.0)
        return jnp.sum(spread.reshape(8, 16, PART), axis=1)

    diagonal = (to_plane(stiff) + (6.0 - SHIFT)) * THETA
    for c in range(3):
        plane = to_plane(flux[c])
        for x in range(8):
            basis[0][(c * 8 + x) * 8 : (c * 8 + x + 1) * 8, :] = source_ref[c, x] - plane

    lane = lax.broadcasted_iota(jnp.int32, (8, PART), 1)
    sub = lax.broadcasted_iota(jnp.int32, (8, PART), 0)
    sides = (
        on_line(lax.rem(gx + NGX - 1, NGX)),
        on_line(lax.rem(gx + 1, NGX)),
        {"gx": gx, "gy": lax.rem(gy + 3, 4), "gz": gz},
        {"gx": gx, "gy": lax.rem(gy + 1, 4), "gz": gz},
        {"gx": gx, "gy": gy, "gz": lax.rem(gz + 3, 4)},
        {"gx": gx, "gy": gy, "gz": lax.rem(gz + 1, 4)},
    )
    starts = (0, FIELDS, 2 * FIELDS, 3 * FIELDS, 4 * FIELDS, 4 * FIELDS + 8)
    sizes = (FIELDS, FIELDS, FIELDS, FIELDS, 8, 8)

    def halo(step, side):
        goal = side + 1 - 2 * (side % 2)
        return pltpu.make_async_remote_copy(
            src_ref=out_halo.at[step, pl.ds(starts[side], sizes[side])],
            dst_ref=in_halo.at[step, pl.ds(starts[goal], sizes[goal])],
            send_sem=send_halo,
            recv_sem=recv_halo.at[step],
            device_id=sides[side],
            device_id_type=MESH,
        )

    def tile(level, n):
        return basis[level][n * 8 : (n + 1) * 8, :]

    def dot(a, b):
        total = tile(a, 0) * tile(b, 0)
        for n in range(1, FIELDS):
            total = total + tile(a, n) * tile(b, n)
        return jnp.sum(jnp.sum(total, axis=0, keepdims=True), axis=1, keepdims=True)

    keep = [
        jnp.where(edge, 0.0, -THETA)
        for edge in (gx == 0, gx == NGX - 1, gy == 0, gy == 3, gz == 0, gz == 3)
    ]
    moments = []

    for step in range(ITERS):
        for c in range(3):
            at = c * 8
            out_halo[step, starts[0] + at : starts[0] + at + 8, :] = tile(step, at)
            out_halo[step, starts[1] + at : starts[1] + at + 8, :] = tile(step, at + 7)
        halo(step, 0).start()
        halo(step, 1).start()
        faces = jnp.zeros((8, PART), F32)
        for n in range(FIELDS):
            turned = pltpu.roll(tile(step, n), 2 * n + 1, 1)
            faces = jnp.where(lane // 2 == n, turned, faces)
        out_halo[step, starts[4] : starts[4] + 8, :] = faces
        out_halo[step, starts[5] : starts[5] + 8, :] = faces
        halo(step, 4).start()
        halo(step, 5).start()
        out_halo[step, starts[2] : starts[3], :] = basis[step][pl.ds(0, FIELDS, stride=8), :]
        out_halo[step, starts[3] : starts[4], :] = basis[step][pl.ds(7, FIELDS, stride=8), :]
        halo(step, 2).start()
        halo(step, 3).start()
        for n in range(FIELDS):
            value = tile(step, n)
            beside = jnp.where(sub == 0, 0.0, pltpu.roll(value, 1, 0))
            beside = beside + jnp.where(sub == 7, 0.0, pltpu.roll(value, 7, 0))
            beside = beside + jnp.where(lane == 0, 0.0, pltpu.roll(value, 1, 1))
            beside = beside + jnp.where(lane == PART - 1, 0.0, pltpu.roll(value, PART - 1, 1))
            if n % 8:
                beside = beside + tile(step, n - 1)
            if n % 8 < 7:
                beside = beside + tile(step, n + 1)
            basis[step + 1][n * 8 : (n + 1) * 8, :] = diagonal * value - THETA * beside
        if step:
            moments.append(dot(step - 1, step))
        moments.append(dot(step, step))
        drain(in_halo.at[step], send_halo, recv_halo.at[step]).wait_recv()
        low = in_halo[step, starts[4] : starts[4] + 8, :] * keep[4]
        high = in_halo[step, starts[5] : starts[5] + 8, :] * keep[5]
        both = jnp.where(lane % 2 == 0, low, pltpu.roll(high, PART - 2, 1))
        for n in range(FIELDS):
            turned = pltpu.roll(both, (PART - 2 * n) % PART, 1)
            more = jnp.where((lane == 0) | (lane == PART - 1), turned, 0.0)
            row_low = in_halo[step, starts[2] + n : starts[2] + n + 1, :] * keep[2]
            row_high = in_halo[step, starts[3] + n : starts[3] + n + 1, :] * keep[3]
            more = more + jnp.where(sub == 0, jnp.broadcast_to(row_low, (8, PART)), 0.0)
            more = more + jnp.where(sub == 7, jnp.broadcast_to(row_high, (8, PART)), 0.0)
            at = n // 8 * 8
            if n % 8 == 0:
                more = more + in_halo[step, starts[0] + at : starts[0] + at + 8, :] * keep[0]
            if n % 8 == 7:
                more = more + in_halo[step, starts[1] + at : starts[1] + at + 8, :] * keep[1]
            basis[step + 1][n * 8 : (n + 1) * 8, :] += more
    moments.append(dot(ITERS - 1, ITERS))

    row = lax.broadcasted_iota(jnp.int32, (1, PART), 1)
    packed = jnp.zeros((1, PART), F32)
    for k, moment in enumerate(moments):
        packed = jnp.where(row == k, moment, packed)

    def all_sum(value, buf, n, turn, device_of):
        buf[0] = value

        def copy(d):
            return pltpu.make_async_remote_copy(
                src_ref=buf.at[0],
                dst_ref=buf.at[n - d],
                send_sem=send_sum.at[turn],
                recv_sem=recv_sum.at[turn],
                device_id=device_of(d),
                device_id_type=MESH,
            )

        for d in sorted(range(1, n), key=lambda d: -min(d, n - d)):
            copy(d).start()
        arrived = drain(buf.at[pl.ds(1, n - 1)], send_sum.at[turn], recv_sum.at[turn])
        arrived.wait_recv()
        return jnp.sum(buf[...], axis=0)

    packed = all_sum(packed, plane_buf, NP, 0, lambda d: on_plane(lax.rem(place + d, NP)))
    total = all_sum(packed, line_buf, NGX, 1, lambda d: on_line(lax.rem(gx + d, NGX)))
    m = [total[:, k : k + 1] for k in range(6)]

    def product(a, b):
        result = None
        for i, left in enumerate(a):
            for j, right in enumerate(b):
                term = left * (right * m[i + j])
                result = term if result is None else result + term
        return result

    unit = jnp.ones((1, 1), F32)
    now = [unit]
    course = [unit]
    taken = []
    norm = m[0]
    for step in range(ITERS):
        image = [SHIFT * course[0]]
        for k in range(1, len(course)):
            image.append(SHIFT * course[k] + (1.0 / THETA) * course[k - 1])
        image.append((1.0 / THETA) * course[-1])
        alpha = norm / product(course, image)
        taken = [
            alpha * g + (taken[k] if k < len(taken) else 0.0) for k, g in enumerate(course)
        ]
        now = [
            (now[k] if k < len(now) else 0.0) - alpha * g for k, g in enumerate(image)
        ]
        if step < ITERS - 1:
            following = product(now, now)
            beta = following / norm
            course = [
                g + (beta * course[k] if k < len(course) else 0.0) for k, g in enumerate(now)
            ]
            norm = following
    for k, g in enumerate(taken + now):
        weights_out[k][...] = jnp.broadcast_to(g, (1, PART))

    drain(column_buf.at[pl.ds(0, NZC - 1)], send_one, recv_one.at[0]).wait_send()
    for half in range(2):
        region = lib.at[half, core, pl.ds(0, NP - 1)]
        drain(region, send_two.at[half], recv_two.at[half]).wait_send()
        three(half, core).wait_send()
    drain(out_halo, send_halo, recv_halo.at[0]).wait_send()
    drain(plane_buf.at[pl.ds(1, NP - 1)], send_sum.at[0], recv_sum.at[0]).wait_send()
    drain(line_buf.at[pl.ds(1, NGX - 1)], send_sum.at[1], recv_sum.at[1]).wait_send()


def per_device(source_field, cell_contrast, point_field, point_class, cell_kind, inverse_blocks):
    vmem = pl.BlockSpec(memory_space=pltpu.VMEM)
    dma = pltpu.SemaphoreType.DMA
    results = pl.pallas_call(
        kernel,
        out_shape=[jax.ShapeDtypeStruct((FIELDS * 8, PART), F32)] * (ITERS + 1)
        + [jax.ShapeDtypeStruct((1, PART), F32)] * (2 * ITERS + 1),
        in_specs=[pl.BlockSpec(memory_space=pltpu.HBM)] * 7,
        out_specs=[vmem] * (3 * ITERS + 2),
        scratch_shapes=[
            pltpu.VMEM(source_field.shape, F32),
            pltpu.VMEM(cell_contrast.shape, BF16),
            pltpu.VMEM(point_field.shape, BF16),
            pltpu.VMEM((1, POINTS), jnp.int32),
            pltpu.VMEM((1, POINTS), jnp.int32),
            pltpu.VMEM((9, TYPES, PART), F32),
            pltpu.VMEM((VOX, VOX), BF16),
            pltpu.VMEM((1, ROW), F32),
            pltpu.VMEM((NZC, 1, ROW), F32),
            pltpu.VMEM((2, 2, NP, 8, SLAB), BF16),
            pltpu.VMEM((4, POINTS, ROW), F32),
            pltpu.VMEM((ITERS, 4 * FIELDS + 16, PART), F32),
            pltpu.VMEM((ITERS, 4 * FIELDS + 16, PART), F32),
            pltpu.VMEM((NP, 1, PART), F32),
            pltpu.VMEM((NGX, 1, PART), F32),
            dma((7,)),
            dma,
            dma((2,)),
            dma((2,)),
            dma((2,)),
            dma((2,)),
            dma((2,)),
            dma,
            dma((ITERS,)),
            dma((2,)),
            dma((2,)),
        ],
        compiler_params=pltpu.CompilerParams(
            collective_id=0, has_side_effects=True, vmem_limit_bytes=40 << 20
        ),
    )(
        *[
            pltpu.with_memory_space_constraint(value, pltpu.HBM)
            for value in (
                source_field,
                cell_contrast,
                point_field,
                point_class.reshape(1, -1),
                cell_kind.reshape(1, -1),
                inverse_blocks.transpose(0, 2, 3, 1, 4).reshape(9, TYPES, VOX),
                jnp.asarray(hartley_table()),
            )
        ]
    )
    shape = source_field.shape
    fields = [field.reshape(shape) for field in results[: ITERS + 1]]
    weights = [weight.reshape(PART) for weight in results[ITERS + 1 :]]
    newton_step = sum(weights[k] * fields[k] for k in range(ITERS))
    residual = sum(weights[ITERS + k] * fields[k] for k in range(ITERS + 1))
    return newton_step, residual


def solution(mesh):
    placed = (
        P(None, "gx", "gy", "gz"),
        P(("gx", "gy", "gz"), None),
        P(None, ("gx", "gy", "gz")),
        P(("gx", "gy", "gz"), None),
        P(("gx", "gy", "gz")),
        P("gx", None, None, None, None),
    )
    return jax.shard_map(
        per_device,
        mesh=mesh,
        in_specs=placed,
        out_specs=(P(None, "gx", "gy", "gz"), P(None, "gx", "gy", "gz")),
        check_vma=False,
    )
```

```python
import functools
import math

import jax
import jax.numpy as jnp
import numpy as np
from jax import lax
from jax.experimental import pallas as pl
from jax.experimental.pallas import tpu as pltpu
from jax.sharding import PartitionSpec as P

CELL = 8
VOX = 512
TYPES = 4
ZP = 8
ITERS = 3
NGX = 32
NZC = 16
NP = 16
OWN = 3
REACH = 4
PART = 128
ROW = 9 * PART
SLAB = ROW + PART
SPLIT = SLAB // 2
POINTS = 128
FIELDS = 24
KERR = 0.1
SHIFT = 7.0
THETA = 2.0**-12

MESH = pl.DeviceIdType.MESH
F32 = jnp.float32
BF16 = jnp.bfloat16


def hartley_table():
    n = np.arange(VOX)
    a, b, c = n // (CELL * CELL), n // CELL % CELL, n % CELL
    phase = (np.outer(a, a) + np.outer(b, b) + np.outer(c, c)) % CELL
    angle = 2.0 * math.pi / CELL * np.arange(CELL)
    values = ((np.cos(angle) + np.sin(angle)) / math.sqrt(VOX)).astype(np.float32)
    values[np.abs(values) < 1e-6] = 0.0
    return values.astype(jnp.bfloat16)[phase]


def kernel(
    source_hbm,
    contrast_hbm,
    point_hbm,
    class_hbm,
    kind_hbm,
    inverse_hbm,
    hartley_hbm,
    level_0,
    level_1,
    level_2,
    level_3,
    weight_0,
    weight_1,
    weight_2,
    weight_3,
    weight_4,
    weight_5,
    weight_6,
    source_ref,
    contrast_ref,
    point_ref,
    class_ref,
    kind_ref,
    inverse_ref,
    hartley_ref,
    slice_buf,
    column_buf,
    lib,
    blocks,
    out_halo,
    in_halo,
    plane_buf,
    line_buf,
    load_sems,
    send_one,
    recv_one,
    send_two,
    recv_two,
    send_three,
    recv_three,
    send_halo,
    recv_halo,
    send_sum,
    recv_sum,
):
    gx, gy, gz = lax.axis_index("gx"), lax.axis_index("gy"), lax.axis_index("gz")
    chip, core = gx // 2, gx % 2
    place = gy * 4 + gz
    basis = (level_0, level_1, level_2, level_3)
    weights_out = (weight_0, weight_1, weight_2, weight_3, weight_4, weight_5, weight_6)

    def on_line(target):
        return {"gx": target, "gy": gy, "gz": gz}

    def on_plane(target):
        return {"gx": gx, "gy": target // 4, "gz": target % 4}

    barrier = pltpu.get_barrier_semaphore()
    near = [d for reach in range(REACH, 0, -1) for d in (reach, NZC - reach)]

    def chip_at(d):
        return on_line(lax.rem(chip + d, NZC) * 2 + core)

    for d in near:
        pl.semaphore_signal(barrier, inc=1, device_id=chip_at(d), device_id_type=MESH)
    for d in range(1, NP):
        pl.semaphore_signal(
            barrier, inc=1, device_id=on_plane(lax.rem(place + d, NP)), device_id_type=MESH
        )
    pl.semaphore_signal(
        barrier, inc=1, device_id=on_line(chip * 2 + 1 - core), device_id_type=MESH
    )

    loads = [
        pltpu.make_async_copy(
            inverse_hbm.at[:, :, pl.ds(pl.multiple_of(gz * PART, PART), PART)],
            inverse_ref,
            load_sems.at[0],
        )
    ]
    pairs = (
        (point_hbm, point_ref),
        (class_hbm, class_ref),
        (kind_hbm, kind_ref),
        (contrast_hbm, contrast_ref),
        (hartley_hbm, hartley_ref),
        (source_hbm, source_ref),
    )
    for n, (origin, goal) in enumerate(pairs):
        loads.append(pltpu.make_async_copy(origin, goal, load_sems.at[n + 1]))
    for load in loads:
        load.start()
    loads[0].wait()

    for n in range(9):
        slice_buf[:, n * PART : (n + 1) * PART] = inverse_ref[n, pl.ds(gy, 1), :]
    column_buf[OWN] = slice_buf[...]

    for load in loads[1:]:
        load.wait()
    rows = lax.broadcasted_iota(jnp.int32, (8, POINTS), 0)
    point = point_ref[...].astype(F32)
    packed = jnp.zeros((8, POINTS), F32)
    entries = [point[i : i + 1] for i in range(3)]
    entries += [kind_ref[...].astype(F32), class_ref[...].astype(F32)]
    for i, entry in enumerate(entries):
        packed = jnp.where(rows == i, jnp.broadcast_to(entry, (8, POINTS)), packed)
    columns = packed.T
    base = [columns[:, i : i + 1] for i in range(3)]
    kind = columns[:, 3:4].astype(jnp.int32)
    owner = columns[:, 4:5].astype(jnp.int32)
    away = (owner // 2 - chip + OWN + NZC) % NZC
    key = (away // 8) * 128 + (owner % 2) * 64 + kind * 16 + away % 8
    depth = lax.broadcasted_iota(jnp.int32, (POINTS, 2 * POINTS), 1)
    hot = [(depth == key + 8 * turn).astype(F32).astype(BF16) for turn in range(2)]
    weights = [contrast_ref[:, i * VOX : (i + 1) * VOX].astype(F32) for i in range(3)]

    def spectrum_of(polar):
        return [
            jnp.dot(polar[i], hartley_ref[...], preferred_element_type=F32) for i in range(3)
        ]

    first = spectrum_of([(weights[i] * base[i]).astype(BF16) for i in range(3)])

    pl.semaphore_wait(barrier, 2 * REACH + NP)

    def one(d):
        return pltpu.make_async_remote_copy(
            src_ref=slice_buf,
            dst_ref=column_buf.at[(OWN - d) % NZC],
            send_sem=send_one.at[0],
            recv_sem=recv_one.at[0],
            device_id=chip_at(d),
            device_id_type=MESH,
        )

    for d in near:
        one(d).start()

    def relay(start, goal, count, d):
        return pltpu.make_async_remote_copy(
            src_ref=column_buf.at[pl.ds(start, count)],
            dst_ref=column_buf.at[pl.ds(goal, count)],
            send_sem=send_one.at[1],
            recv_sem=recv_one.at[1],
            device_id=chip_at(d),
            device_id_type=MESH,
        )

    def drain(region, send_sem, recv_sem):
        return pltpu.make_async_remote_copy(
            src_ref=region,
            dst_ref=region,
            send_sem=send_sem,
            recv_sem=recv_sem,
            device_id=on_line(chip * 2 + 1 - core),
            device_id_type=MESH,
        )

    def two(half, d):
        at = lib.at[half, core, place]
        return pltpu.make_async_remote_copy(
            src_ref=at,
            dst_ref=at,
            send_sem=send_two.at[half],
            recv_sem=recv_two.at[half],
            device_id=on_plane(lax.rem(place + d, NP)),
            device_id_type=MESH,
        )

    def three(half, which):
        return drain(lib.at[half, which], send_three.at[half], recv_three.at[half])

    lanes = lax.broadcasted_iota(jnp.int32, (8, PART), 1)
    for half in range(2):
        taken = drain(column_buf.at[pl.ds(0, 8 - half)], send_one.at[half], recv_one.at[half])
        taken.wait_recv()
        if half == 0:
            relay(4, 8, 4, NZC - REACH).start()
            relay(0, 12, 3, REACH).start()
        wide = column_buf[half * 8 : (half + 1) * 8].reshape(8, ROW)
        rest = wide - wide.astype(BF16).astype(F32)
        tail = jnp.zeros((8, PART), F32)
        for n in range(9):
            lead = jnp.broadcast_to(rest[:, n * PART : n * PART + 1], (8, PART))
            tail = jnp.where(lanes == n, lead, tail)
        ends = jnp.concatenate([wide[:, SPLIT:ROW], tail], axis=1)
        pair = jnp.concatenate([wide[:, 0:SPLIT], ends], axis=0)
        lib[half, core, place] = pair.astype(BF16)
        for d in range(1, NP):
            two(half, d).start()

    for half in range(2):
        region = lib.at[half, core, pl.ds(0, NP - 1)]
        drain(region, send_two.at[half], recv_two.at[half]).wait_recv()
        three(half, core).start()
    for half in range(2):
        three(half, 1 - core).wait_recv()

    for f in range(4):
        part = jnp.concatenate(
            [lib[half, c, k * 4 + f] for half in range(2) for c in range(2) for k in range(4)],
            axis=0,
        )
        chosen = jnp.concatenate(
            [jnp.dot(pick, part, preferred_element_type=F32) for pick in hot], axis=1
        )
        if f:
            blocks[f] = chosen[:, 0:ROW]
        else:
            lead = lax.broadcasted_iota(jnp.int32, (POINTS, PART), 1) == 0
            for n in range(9):
                tail = jnp.broadcast_to(chosen[:, ROW + n : ROW + n + 1], (POINTS, PART))
                blocks[f, :, n * PART : (n + 1) * PART] = chosen[
                    :, n * PART : (n + 1) * PART
                ] + jnp.where(lead, tail, 0.0)

    def correction(spectrum):
        mixed = []
        for i in range(3):
            parts = []
            for f in range(4):
                total = None
                for j in range(3):
                    at = (i * 3 + j) * PART
                    term = (
                        blocks[f, :, at : at + PART]
                        * spectrum[j][:, f * PART : (f + 1) * PART]
                    )
                    total = term if total is None else total + term
                parts.append(total.astype(BF16))
            mixed.append(jnp.concatenate(parts, axis=1))
        return spectrum_of(mixed)

    local = [base[i] - c for i, c in enumerate(correction(first))]
    polar = [
        (weights[i] * local[i] * (1.0 + KERR * local[i] * local[i])).astype(BF16)
        for i in range(3)
    ]
    final = [base[i] - c for i, c in enumerate(correction(spectrum_of(polar)))]
    flux = [
        jnp.sum((1.0 + weights[i]) * final[i], axis=1, keepdims=True) * (1.0 / VOX)
        for i in range(3)
    ]
    energy = sum(weights[i] * final[i] * final[i] for i in range(3))
    stiff = 0.5 + jnp.sum(energy, axis=1, keepdims=True) * (1.0 / (3 * VOX))

    q = lax.broadcasted_iota(jnp.int32, (POINTS, PART), 0)
    z = lax.broadcasted_iota(jnp.int32, (POINTS, PART), 1)
    here = (q % 16) == (z // ZP)

    def to_plane(column):
        spread = jnp.where(here, jnp.broadcast_to(column, (POINTS, PART)), 0.0)
        return jnp.sum(spread.reshape(8, 16, PART), axis=1)

    diagonal = (to_plane(stiff) + (6.0 - SHIFT)) * THETA
    for c in range(3):
        plane = to_plane(flux[c])
        for x in range(8):
            basis[0][(c * 8 + x) * 8 : (c * 8 + x + 1) * 8, :] = source_ref[c, x] - plane

    lane = lax.broadcasted_iota(jnp.int32, (8, PART), 1)
    sub = lax.broadcasted_iota(jnp.int32, (8, PART), 0)
    sides = (
        on_line(lax.rem(gx + NGX - 1, NGX)),
        on_line(lax.rem(gx + 1, NGX)),
        {"gx": gx, "gy": lax.rem(gy + 3, 4), "gz": gz},
        {"gx": gx, "gy": lax.rem(gy + 1, 4), "gz": gz},
        {"gx": gx, "gy": gy, "gz": lax.rem(gz + 3, 4)},
        {"gx": gx, "gy": gy, "gz": lax.rem(gz + 1, 4)},
    )
    starts = (0, FIELDS, 2 * FIELDS, 3 * FIELDS, 4 * FIELDS, 4 * FIELDS + 8)
    sizes = (FIELDS, FIELDS, FIELDS, FIELDS, 8, 8)

    def halo(step, side):
        goal = side + 1 - 2 * (side % 2)
        return pltpu.make_async_remote_copy(
            src_ref=out_halo.at[step, pl.ds(starts[side], sizes[side])],
            dst_ref=in_halo.at[step, pl.ds(starts[goal], sizes[goal])],
            send_sem=send_halo,
            recv_sem=recv_halo.at[step],
            device_id=sides[side],
            device_id_type=MESH,
        )

    def tile(level, n):
        return basis[level][n * 8 : (n + 1) * 8, :]

    def dot(a, b):
        total = tile(a, 0) * tile(b, 0)
        for n in range(1, FIELDS):
            total = total + tile(a, n) * tile(b, n)
        return jnp.sum(jnp.sum(total, axis=0, keepdims=True), axis=1, keepdims=True)

    keep = [
        jnp.where(edge, 0.0, -THETA)
        for edge in (gx == 0, gx == NGX - 1, gy == 0, gy == 3, gz == 0, gz == 3)
    ]
    moments = []

    for step in range(ITERS):
        for c in range(3):
            at = c * 8
            out_halo[step, starts[0] + at : starts[0] + at + 8, :] = tile(step, at)
            out_halo[step, starts[1] + at : starts[1] + at + 8, :] = tile(step, at + 7)
        halo(step, 0).start()
        halo(step, 1).start()
        faces = jnp.zeros((8, PART), F32)
        for n in range(FIELDS):
            turned = pltpu.roll(tile(step, n), 2 * n + 1, 1)
            faces = jnp.where(lane // 2 == n, turned, faces)
        out_halo[step, starts[4] : starts[4] + 8, :] = faces
        out_halo[step, starts[5] : starts[5] + 8, :] = faces
        halo(step, 4).start()
        halo(step, 5).start()
        out_halo[step, starts[2] : starts[3], :] = basis[step][pl.ds(0, FIELDS, stride=8), :]
        out_halo[step, starts[3] : starts[4], :] = basis[step][pl.ds(7, FIELDS, stride=8), :]
        halo(step, 2).start()
        halo(step, 3).start()
        for n in range(FIELDS):
            value = tile(step, n)
            beside = jnp.where(sub == 0, 0.0, pltpu.roll(value, 1, 0))
            beside = beside + jnp.where(sub == 7, 0.0, pltpu.roll(value, 7, 0))
            beside = beside + jnp.where(lane == 0, 0.0, pltpu.roll(value, 1, 1))
            beside = beside + jnp.where(lane == PART - 1, 0.0, pltpu.roll(value, PART - 1, 1))
            if n % 8:
                beside = beside + tile(step, n - 1)
            if n % 8 < 7:
                beside = beside + tile(step, n + 1)
            basis[step + 1][n * 8 : (n + 1) * 8, :] = diagonal * value - THETA * beside
        if step:
            moments.append(dot(step - 1, step))
        moments.append(dot(step, step))
        drain(in_halo.at[step], send_halo, recv_halo.at[step]).wait_recv()
        low = in_halo[step, starts[4] : starts[4] + 8, :] * keep[4]
        high = in_halo[step, starts[5] : starts[5] + 8, :] * keep[5]
        both = jnp.where(lane % 2 == 0, low, pltpu.roll(high, PART - 2, 1))
        for n in range(FIELDS):
            turned = pltpu.roll(both, (PART - 2 * n) % PART, 1)
            more = jnp.where((lane == 0) | (lane == PART - 1), turned, 0.0)
            row_low = in_halo[step, starts[2] + n : starts[2] + n + 1, :] * keep[2]
            row_high = in_halo[step, starts[3] + n : starts[3] + n + 1, :] * keep[3]
            more = more + jnp.where(sub == 0, jnp.broadcast_to(row_low, (8, PART)), 0.0)
            more = more + jnp.where(sub == 7, jnp.broadcast_to(row_high, (8, PART)), 0.0)
            at = n // 8 * 8
            if n % 8 == 0:
                more = more + in_halo[step, starts[0] + at : starts[0] + at + 8, :] * keep[0]
            if n % 8 == 7:
                more = more + in_halo[step, starts[1] + at : starts[1] + at + 8, :] * keep[1]
            basis[step + 1][n * 8 : (n + 1) * 8, :] += more
    moments.append(dot(ITERS - 1, ITERS))

    row = lax.broadcasted_iota(jnp.int32, (1, PART), 1)
    packed = jnp.zeros((1, PART), F32)
    for k, moment in enumerate(moments):
        packed = jnp.where(row == k, moment, packed)

    def all_sum(value, buf, n, turn, device_of):
        buf[0] = value

        def copy(d):
            return pltpu.make_async_remote_copy(
                src_ref=buf.at[0],
                dst_ref=buf.at[n - d],
                send_sem=send_sum.at[turn],
                recv_sem=recv_sum.at[turn],
                device_id=device_of(d),
                device_id_type=MESH,
            )

        for d in sorted(range(1, n), key=lambda d: -min(d, n - d)):
            copy(d).start()
        arrived = drain(buf.at[pl.ds(1, n - 1)], send_sum.at[turn], recv_sum.at[turn])
        arrived.wait_recv()
        return jnp.sum(buf[...], axis=0)

    packed = all_sum(packed, plane_buf, NP, 0, lambda d: on_plane(lax.rem(place + d, NP)))
    total = all_sum(packed, line_buf, NGX, 1, lambda d: on_line(lax.rem(gx + d, NGX)))
    m = [total[:, k : k + 1] for k in range(6)]

    def product(a, b):
        result = None
        for i, left in enumerate(a):
            for j, right in enumerate(b):
                term = left * (right * m[i + j])
                result = term if result is None else result + term
        return result

    unit = jnp.ones((1, 1), F32)
    now = [unit]
    course = [unit]
    taken = []
    norm = m[0]
    for step in range(ITERS):
        image = [SHIFT * course[0]]
        for k in range(1, len(course)):
            image.append(SHIFT * course[k] + (1.0 / THETA) * course[k - 1])
        image.append((1.0 / THETA) * course[-1])
        alpha = norm / product(course, image)
        taken = [
            alpha * g + (taken[k] if k < len(taken) else 0.0) for k, g in enumerate(course)
        ]
        now = [
            (now[k] if k < len(now) else 0.0) - alpha * g for k, g in enumerate(image)
        ]
        if step < ITERS - 1:
            following = product(now, now)
            beta = following / norm
            course = [
                g + (beta * course[k] if k < len(course) else 0.0) for k, g in enumerate(now)
            ]
            norm = following
    for k, g in enumerate(taken + now):
        weights_out[k][...] = jnp.broadcast_to(g, (1, PART))

    for half in range(2):
        region = column_buf.at[pl.ds(0, 8 - half)]
        drain(region, send_one.at[half], recv_one.at[half]).wait_send()
        region = lib.at[half, core, pl.ds(0, NP - 1)]
        drain(region, send_two.at[half], recv_two.at[half]).wait_send()
        three(half, core).wait_send()
    drain(out_halo, send_halo, recv_halo.at[0]).wait_send()
    drain(plane_buf.at[pl.ds(1, NP - 1)], send_sum.at[0], recv_sum.at[0]).wait_send()
    drain(line_buf.at[pl.ds(1, NGX - 1)], send_sum.at[1], recv_sum.at[1]).wait_send()


def per_device(source_field, cell_contrast, point_field, point_class, cell_kind, inverse_blocks):
    vmem = pl.BlockSpec(memory_space=pltpu.VMEM)
    dma = pltpu.SemaphoreType.DMA
    results = pl.pallas_call(
        kernel,
        out_shape=[jax.ShapeDtypeStruct((FIELDS * 8, PART), F32)] * (ITERS + 1)
        + [jax.ShapeDtypeStruct((1, PART), F32)] * (2 * ITERS + 1),
        in_specs=[pl.BlockSpec(memory_space=pltpu.HBM)] * 7,
        out_specs=[vmem] * (3 * ITERS + 2),
        scratch_shapes=[
            pltpu.VMEM(source_field.shape, F32),
            pltpu.VMEM(cell_contrast.shape, BF16),
            pltpu.VMEM(point_field.shape, BF16),
            pltpu.VMEM((1, POINTS), jnp.int32),
            pltpu.VMEM((1, POINTS), jnp.int32),
            pltpu.VMEM((9, TYPES, PART), F32),
            pltpu.VMEM((VOX, VOX), BF16),
            pltpu.VMEM((1, ROW), F32),
            pltpu.VMEM((NZC, 1, ROW), F32),
            pltpu.VMEM((2, 2, NP, 16, SPLIT), BF16),
            pltpu.VMEM((4, POINTS, ROW), F32),
            pltpu.VMEM((ITERS, 4 * FIELDS + 16, PART), F32),
            pltpu.VMEM((ITERS, 4 * FIELDS + 16, PART), F32),
            pltpu.VMEM((NP, 1, PART), F32),
            pltpu.VMEM((NGX, 1, PART), F32),
            dma((7,)),
            dma((2,)),
            dma((2,)),
            dma((2,)),
            dma((2,)),
            dma((2,)),
            dma((2,)),
            dma,
            dma((ITERS,)),
            dma((2,)),
            dma((2,)),
        ],
        compiler_params=pltpu.CompilerParams(
            collective_id=0, has_side_effects=True, vmem_limit_bytes=40 << 20
        ),
    )(
        *[
            pltpu.with_memory_space_constraint(value, pltpu.HBM)
            for value in (
                source_field,
                cell_contrast,
                point_field,
                point_class.reshape(1, -1),
                cell_kind.reshape(1, -1),
                inverse_blocks.transpose(0, 2, 3, 1, 4).reshape(9, TYPES, VOX),
                jnp.asarray(hartley_table()),
            )
        ]
    )
    shape = source_field.shape
    fields = [field.reshape(shape) for field in results[: ITERS + 1]]
    weights = [weight.reshape(PART) for weight in results[ITERS + 1 :]]
    newton_step = sum(weights[k] * fields[k] for k in range(ITERS))
    residual = sum(weights[ITERS + k] * fields[k] for k in range(ITERS + 1))
    return newton_step, residual


def solution(mesh):
    placed = (
        P(None, "gx", "gy", "gz"),
        P(("gx", "gy", "gz"), None),
        P(None, ("gx", "gy", "gz")),
        P(("gx", "gy", "gz"), None),
        P(("gx", "gy", "gz")),
        P("gx", None, None, None, None),
    )
    return jax.shard_map(
        per_device,
        mesh=mesh,
        in_specs=placed,
        out_specs=(P(None, "gx", "gy", "gz"), P(None, "gx", "gy", "gz")),
        check_vma=False,
    )
```

```python
import functools
import math

import jax
import jax.numpy as jnp
import numpy as np
from jax import lax
from jax.experimental import pallas as pl
from jax.experimental.pallas import tpu as pltpu
from jax.sharding import PartitionSpec as P

CELL = 8
VOX = 512
TYPES = 4
ZP = 8
ITERS = 3
NGX = 32
NZC = 16
NP = 16
OWN = 3
REACH = 4
WIDE = 56
IN_XY = 4 * WIDE + 32
IN_XZ = IN_XY + 4 * 24
IN_YZ = IN_XZ + 32
PART = 128
ROW = 9 * PART
SLAB = ROW + PART
SPLIT = SLAB // 2
POINTS = 128
FIELDS = 24
KERR = 0.1
SHIFT = 7.0
THETA = 2.0**-12

MESH = pl.DeviceIdType.MESH
F32 = jnp.float32
BF16 = jnp.bfloat16


def hartley_table():
    n = np.arange(VOX)
    a, b, c = n // (CELL * CELL), n // CELL % CELL, n % CELL
    phase = (np.outer(a, a) + np.outer(b, b) + np.outer(c, c)) % CELL
    angle = 2.0 * math.pi / CELL * np.arange(CELL)
    values = ((np.cos(angle) + np.sin(angle)) / math.sqrt(VOX)).astype(np.float32)
    values[np.abs(values) < 1e-6] = 0.0
    return values.astype(jnp.bfloat16)[phase]


def kernel(
    source_hbm,
    contrast_hbm,
    point_hbm,
    class_hbm,
    kind_hbm,
    inverse_hbm,
    hartley_hbm,
    level_0,
    level_1,
    level_2,
    level_3,
    weight_0,
    weight_1,
    weight_2,
    weight_3,
    weight_4,
    weight_5,
    weight_6,
    source_ref,
    contrast_ref,
    point_ref,
    class_ref,
    kind_ref,
    inverse_ref,
    hartley_ref,
    slice_buf,
    column_buf,
    lib,
    blocks,
    out_halo,
    in_halo,
    wide_out,
    wide_in,
    plane_buf,
    line_buf,
    load_sems,
    send_one,
    recv_one,
    send_two,
    recv_two,
    send_three,
    recv_three,
    send_halo,
    recv_halo,
    send_wide,
    recv_wide,
    send_sum,
    recv_sum,
):
    gx, gy, gz = lax.axis_index("gx"), lax.axis_index("gy"), lax.axis_index("gz")
    chip, core = gx // 2, gx % 2
    place = gy * 4 + gz
    basis = (level_0, level_1, level_2, level_3)
    weights_out = (weight_0, weight_1, weight_2, weight_3, weight_4, weight_5, weight_6)

    def on_line(target):
        return {"gx": target, "gy": gy, "gz": gz}

    def ring(d):
        return min(d, 4 - d)

    plane_steps = sorted(
        range(1, NP), key=lambda d: (-ring(d // 4) - ring(d % 4), d)
    )

    def plane_at(d):
        return {"gx": gx, "gy": lax.rem(gy + d // 4, 4), "gz": lax.rem(gz + d % 4, 4)}

    def opposite(d):
        return (4 - d // 4) % 4 * 4 + (4 - d % 4) % 4

    barrier = pltpu.get_barrier_semaphore()
    near = [d for reach in range(REACH, 0, -1) for d in (reach, NZC - reach)]

    def chip_at(d):
        return on_line(lax.rem(chip + d, NZC) * 2 + core)

    for d in near:
        pl.semaphore_signal(barrier, inc=1, device_id=chip_at(d), device_id_type=MESH)
    for d in plane_steps:
        pl.semaphore_signal(barrier, inc=1, device_id=plane_at(d), device_id_type=MESH)
    pl.semaphore_signal(
        barrier, inc=1, device_id=on_line(chip * 2 + 1 - core), device_id_type=MESH
    )

    loads = [
        pltpu.make_async_copy(
            inverse_hbm.at[:, :, pl.ds(pl.multiple_of(gz * PART, PART), PART)],
            inverse_ref,
            load_sems.at[0],
        )
    ]
    pairs = (
        (point_hbm, point_ref),
        (class_hbm, class_ref),
        (kind_hbm, kind_ref),
        (contrast_hbm, contrast_ref),
        (hartley_hbm, hartley_ref),
        (source_hbm, source_ref),
    )
    for n, (origin, goal) in enumerate(pairs):
        loads.append(pltpu.make_async_copy(origin, goal, load_sems.at[n + 1]))
    for load in loads:
        load.start()
    loads[0].wait()

    for n in range(9):
        slice_buf[:, n * PART : (n + 1) * PART] = inverse_ref[n, pl.ds(gy, 1), :]
    column_buf[OWN] = slice_buf[...]

    pl.semaphore_wait(barrier, 2 * REACH + NP)

    def one(d):
        return pltpu.make_async_remote_copy(
            src_ref=slice_buf,
            dst_ref=column_buf.at[(OWN - d) % NZC],
            send_sem=send_one.at[0],
            recv_sem=recv_one.at[0],
            device_id=chip_at(d),
            device_id_type=MESH,
        )

    for d in near:
        one(d).start()

    for load in loads[1:]:
        load.wait()
    rows = lax.broadcasted_iota(jnp.int32, (8, POINTS), 0)
    point = point_ref[...].astype(F32)
    packed = jnp.zeros((8, POINTS), F32)
    entries = [point[i : i + 1] for i in range(3)]
    entries += [kind_ref[...].astype(F32), class_ref[...].astype(F32)]
    for i, entry in enumerate(entries):
        packed = jnp.where(rows == i, jnp.broadcast_to(entry, (8, POINTS)), packed)
    columns = packed.T
    base = [columns[:, i : i + 1] for i in range(3)]
    kind = columns[:, 3:4].astype(jnp.int32)
    owner = columns[:, 4:5].astype(jnp.int32)
    away = (owner // 2 - chip + OWN + NZC) % NZC
    key = (away // 8) * 128 + (owner % 2) * 64 + kind * 16 + away % 8
    depth = lax.broadcasted_iota(jnp.int32, (POINTS, 2 * POINTS), 1)
    hot = [(depth == key + 8 * turn).astype(F32).astype(BF16) for turn in range(2)]
    weights = [contrast_ref[:, i * VOX : (i + 1) * VOX].astype(F32) for i in range(3)]

    def spectrum_of(polar):
        return [
            jnp.dot(polar[i], hartley_ref[...], preferred_element_type=F32) for i in range(3)
        ]

    first = spectrum_of([(weights[i] * base[i]).astype(BF16) for i in range(3)])

    def relay(start, goal, count, d):
        return pltpu.make_async_remote_copy(
            src_ref=column_buf.at[pl.ds(start, count)],
            dst_ref=column_buf.at[pl.ds(goal, count)],
            send_sem=send_one.at[1],
            recv_sem=recv_one.at[1],
            device_id=chip_at(d),
            device_id_type=MESH,
        )

    def drain(region, send_sem, recv_sem):
        return pltpu.make_async_remote_copy(
            src_ref=region,
            dst_ref=region,
            send_sem=send_sem,
            recv_sem=recv_sem,
            device_id=on_line(chip * 2 + 1 - core),
            device_id_type=MESH,
        )

    def two(half, d):
        at = lib.at[half, core, place]
        return pltpu.make_async_remote_copy(
            src_ref=at,
            dst_ref=at,
            send_sem=send_two.at[half],
            recv_sem=recv_two.at[half],
            device_id=plane_at(d),
            device_id_type=MESH,
        )

    def three(half, which):
        return drain(lib.at[half, which], send_three.at[half], recv_three.at[half])

    lanes = lax.broadcasted_iota(jnp.int32, (8, PART), 1)
    for half in range(2):
        taken = drain(column_buf.at[pl.ds(0, 8 - half)], send_one.at[half], recv_one.at[half])
        taken.wait_recv()
        if half == 0:
            relay(4, 8, 4, NZC - REACH).start()
            relay(0, 12, 3, REACH).start()
        wide = column_buf[half * 8 : (half + 1) * 8].reshape(8, ROW)
        rest = wide - wide.astype(BF16).astype(F32)
        tail = jnp.zeros((8, PART), F32)
        for n in range(9):
            lead = jnp.broadcast_to(rest[:, n * PART : n * PART + 1], (8, PART))
            tail = jnp.where(lanes == n, lead, tail)
        ends = jnp.concatenate([wide[:, SPLIT:ROW], tail], axis=1)
        pair = jnp.concatenate([wide[:, 0:SPLIT], ends], axis=0)
        lib[half, core, place] = pair.astype(BF16)
        for d in plane_steps:
            two(half, d).start()

    for half in range(2):
        region = lib.at[half, core, pl.ds(0, NP - 1)]
        drain(region, send_two.at[half], recv_two.at[half]).wait_recv()
        three(half, core).start()
    for half in range(2):
        three(half, 1 - core).wait_recv()

    for f in range(4):
        part = jnp.concatenate(
            [lib[half, c, k * 4 + f] for half in range(2) for c in range(2) for k in range(4)],
            axis=0,
        )
        chosen = jnp.concatenate(
            [jnp.dot(pick, part, preferred_element_type=F32) for pick in hot], axis=1
        )
        if f:
            blocks[f] = chosen[:, 0:ROW]
        else:
            lead = lax.broadcasted_iota(jnp.int32, (POINTS, PART), 1) == 0
            for n in range(9):
                tail = jnp.broadcast_to(chosen[:, ROW + n : ROW + n + 1], (POINTS, PART))
                blocks[f, :, n * PART : (n + 1) * PART] = chosen[
                    :, n * PART : (n + 1) * PART
                ] + jnp.where(lead, tail, 0.0)

    def correction(spectrum):
        mixed = []
        for i in range(3):
            parts = []
            for f in range(4):
                total = None
                for j in range(3):
                    at = (i * 3 + j) * PART
                    term = (
                        blocks[f, :, at : at + PART]
                        * spectrum[j][:, f * PART : (f + 1) * PART]
                    )
                    total = term if total is None else total + term
                parts.append(total.astype(BF16))
            mixed.append(jnp.concatenate(parts, axis=1))
        return spectrum_of(mixed)

    local = [base[i] - c for i, c in enumerate(correction(first))]
    polar = [
        (weights[i] * local[i] * (1.0 + KERR * local[i] * local[i])).astype(BF16)
        for i in range(3)
    ]
    final = [base[i] - c for i, c in enumerate(correction(spectrum_of(polar)))]
    flux = [
        jnp.sum((1.0 + weights[i]) * final[i], axis=1, keepdims=True) * (1.0 / VOX)
        for i in range(3)
    ]
    energy = sum(weights[i] * final[i] * final[i] for i in range(3))
    stiff = 0.5 + jnp.sum(energy, axis=1, keepdims=True) * (1.0 / (3 * VOX))

    q = lax.broadcasted_iota(jnp.int32, (POINTS, PART), 0)
    z = lax.broadcasted_iota(jnp.int32, (POINTS, PART), 1)
    here = (q % 16) == (z // ZP)

    def to_plane(column):
        spread = jnp.where(here, jnp.broadcast_to(column, (POINTS, PART)), 0.0)
        return jnp.sum(spread.reshape(8, 16, PART), axis=1)

    diagonal = (to_plane(stiff) + (6.0 - SHIFT)) * THETA
    for c in range(3):
        plane = to_plane(flux[c])
        for x in range(8):
            basis[0][(c * 8 + x) * 8 : (c * 8 + x + 1) * 8, :] = source_ref[c, x] - plane

    lane = lax.broadcasted_iota(jnp.int32, (8, PART), 1)
    sub = lax.broadcasted_iota(jnp.int32, (8, PART), 0)
    sides = (
        on_line(lax.rem(gx + NGX - 1, NGX)),
        on_line(lax.rem(gx + 1, NGX)),
        {"gx": gx, "gy": lax.rem(gy + 3, 4), "gz": gz},
        {"gx": gx, "gy": lax.rem(gy + 1, 4), "gz": gz},
        {"gx": gx, "gy": gy, "gz": lax.rem(gz + 3, 4)},
        {"gx": gx, "gy": gy, "gz": lax.rem(gz + 1, 4)},
    )
    starts = (0, FIELDS, 2 * FIELDS, 3 * FIELDS, 4 * FIELDS, 4 * FIELDS + 8)
    sizes = (FIELDS, FIELDS, FIELDS, FIELDS, 8, 8)

    def halo(step, side):
        goal = side + 1 - 2 * (side % 2)
        return pltpu.make_async_remote_copy(
            src_ref=out_halo.at[step, pl.ds(starts[side], sizes[side])],
            dst_ref=in_halo.at[step, pl.ds(starts[goal], sizes[goal])],
            send_sem=send_halo,
            recv_sem=recv_halo.at[step],
            device_id=sides[side],
            device_id_type=MESH,
        )

    def tile(level, n):
        return basis[level][n * 8 : (n + 1) * 8, :]

    def dot(a, b):
        total = tile(a, 0) * tile(b, 0)
        for n in range(1, FIELDS):
            total = total + tile(a, n) * tile(b, n)
        return jnp.sum(jnp.sum(total, axis=0, keepdims=True), axis=1, keepdims=True)

    keep = [
        jnp.where(edge, 0.0, -THETA)
        for edge in (gx == 0, gx == NGX - 1, gy == 0, gy == 3, gz == 0, gz == 3)
    ]
    moments = []

    def around(dx, dy, dz):
        return {
            "gx": lax.rem(gx + dx + NGX, NGX),
            "gy": lax.rem(gy + dy + 4, 4),
            "gz": lax.rem(gz + dz + 4, 4),
        }

    ends = (-1, 1)
    inside = [
        [jnp.where(edge, 0.0, 1.0) for edge in pair]
        for pair in ((gx == 0, gx == NGX - 1), (gy == 0, gy == 3), (gz == 0, gz == 3))
    ]

    def turn_faces(values, first, last):
        faces = jnp.zeros((8, PART), F32)
        for n, value in enumerate(values):
            at_low = pltpu.roll(value, (2 * n + 1 + last) % PART, 1)
            at_high = at_low
            if first or last:
                at_high = pltpu.roll(value, (2 * n + 1 - first) % PART, 1)
            faces = jnp.where(lane == 2 * n, at_low, jnp.where(lane == 2 * n + 1, at_high, faces))
        return faces

    def start_wide(group):
        rows, lines, edges, faces = [], [], [], []
        for e in range(2):
            o = 1 - e
            lines.append((e * WIDE, WIDE, o * WIDE, around(ends[e], 0, 0)))
            lines.append(((2 + e) * WIDE, WIDE, (2 + o) * WIDE, around(0, ends[e], 0)))
            faces.append((4 * WIDE, 16, 4 * WIDE + 16 * o, around(0, 0, ends[e])))
        for e in range(2):
            for g in range(2):
                slot = (1 - e) * 2 + 1 - g
                rows.append(
                    ((2 + g) * WIDE, FIELDS, IN_XY + slot * FIELDS, around(ends[e], ends[g], 0))
                )
                edges.append((4 * WIDE, 8, IN_XZ + slot * 8, around(ends[e], 0, ends[g])))
                edges.append((4 * WIDE, 8, IN_YZ + slot * 8, around(0, ends[e], ends[g])))
        for origin, size, goal, target in (rows, lines, edges, faces)[group]:
            pltpu.make_async_remote_copy(
                src_ref=wide_out.at[pl.ds(origin, size)],
                dst_ref=wide_in.at[pl.ds(goal, size)],
                send_sem=send_wide,
                recv_sem=recv_wide,
                device_id=target,
                device_id_type=MESH,
            ).start()

    def send_wide_halo():
        for e, (near_y, next_y) in enumerate(((0, 1), (7, 6))):
            at = (2 + e) * WIDE
            wide_out[at : at + 24, :] = basis[0][pl.ds(near_y, FIELDS, stride=8), :]
            wide_out[at + 24 : at + 48, :] = basis[0][pl.ds(next_y, FIELDS, stride=8), :]
            wide_out[at + 48 : at + 56, :] = jnp.broadcast_to(
                diagonal[near_y : near_y + 1], (8, PART)
            )
        start_wide(0)
        for e, (near_x, next_x) in enumerate(((0, 1), (7, 6))):
            at = e * WIDE
            for c in range(3):
                wide_out[at + c * 8 : at + c * 8 + 8, :] = tile(0, c * 8 + near_x)
                wide_out[at + 24 + c * 8 : at + 32 + c * 8, :] = tile(0, c * 8 + next_x)
            wide_out[at + 48 : at + 56, :] = diagonal
        start_wide(1)
        values = [tile(0, n) for n in range(FIELDS)]
        wide_out[4 * WIDE : 4 * WIDE + 8, :] = turn_faces(values + [diagonal], 0, 0)
        start_wide(2)
        wide_out[4 * WIDE + 8 : 4 * WIDE + 16, :] = turn_faces(values, 1, 1)
        start_wide(3)

    def spread_row(value):
        return jnp.broadcast_to(value, (8, PART))

    def image_on_faces():
        even = lane % 2 == 0

        def part(at, size=8):
            return wide_in[at : at + size, :]

        def corner_rows(e, g, n):
            at = IN_XY + (e * 2 + g) * FIELDS + n
            return wide_in[at : at + 1, :] * inside[0][e] * inside[1][g]

        def mixed(at, low, high):
            return jnp.where(even, part(at) * low, part(at + 8) * high)

        xz = [mixed(IN_XZ + 16 * e, *inside[2]) * inside[0][e] for e in range(2)]
        yz = [mixed(IN_YZ + 16 * e, *inside[2]) * inside[1][e] for e in range(2)]
        for e in range(2):
            n_at = 7 if e == 0 else 0
            at = e * WIDE
            own_x = 0 if e == 0 else 7
            for c in range(3):
                value = part(at + c * 8)
                n = c * 8 + n_at
                beside = part(at + 24 + c * 8) + tile(0, c * 8 + own_x)
                beside = beside + jnp.where(
                    sub == 0, spread_row(corner_rows(e, 0, n)), pltpu.roll(value, 1, 0)
                )
                beside = beside + jnp.where(
                    sub == 7, spread_row(corner_rows(e, 1, n)), pltpu.roll(value, 7, 0)
                )
                beside = beside + jnp.where(
                    lane == 0,
                    pltpu.roll(xz[e], (PART - 2 * n) % PART, 1),
                    pltpu.roll(value, 1, 1),
                )
                beside = beside + jnp.where(
                    lane == PART - 1,
                    pltpu.roll(xz[e], (PART - 2 - 2 * n) % PART, 1),
                    pltpu.roll(value, PART - 1, 1),
                )
                image = part(at + 48) * value - THETA * beside
                goal = starts[e] + c * 8
                in_halo[1, goal : goal + 8, :] = image * inside[0][e]
            at = (2 + e) * WIDE
            row_at = 7 if e == 0 else 0
            edge = spread_row(yz[e][row_at : row_at + 1])
            for c in range(3):
                value = part(at + c * 8)
                own = wide_out[at + c * 8 : at + c * 8 + 8, :]
                beside = part(at + 24 + c * 8) + own
                beside = beside + jnp.where(
                    sub == 0, spread_row(corner_rows(0, e, c * 8 + 7)), pltpu.roll(value, 1, 0)
                )
                beside = beside + jnp.where(
                    sub == 7, spread_row(corner_rows(1, e, c * 8)), pltpu.roll(value, 7, 0)
                )
                lanes_low = 2 * (c * 8 + sub)
                low = jnp.sum(jnp.where(lane == lanes_low, edge, 0.0), axis=1, keepdims=True)
                high = jnp.sum(jnp.where(lane == lanes_low + 1, edge, 0.0), axis=1, keepdims=True)
                beside = beside + jnp.where(
                    lane == 0, jnp.broadcast_to(low, (8, PART)), pltpu.roll(value, 1, 1)
                )
                beside = beside + jnp.where(
                    lane == PART - 1,
                    jnp.broadcast_to(high, (8, PART)),
                    pltpu.roll(value, PART - 1, 1),
                )
                image = part(at + 48) * value - THETA * beside
                goal = starts[2 + e] + c * 8
                in_halo[1, goal : goal + 8, :] = image * inside[1][e]
        at = 4 * WIDE
        value = jnp.where(even, part(at), part(at + 16))
        beyond = jnp.where(even, part(at + 8), part(at + 24))
        faces = wide_out[at : at + 8, :]
        own = jnp.where(even, pltpu.roll(faces, PART - 1, 1), pltpu.roll(faces, 1, 1))
        weight = jnp.where(
            even,
            jnp.broadcast_to(part(at)[:, 48:49], (8, PART)),
            jnp.broadcast_to(part(at + 16)[:, 49:50], (8, PART)),
        )
        beside = beyond + own
        beside = beside + jnp.where(
            sub == 0, pltpu.roll(yz[0], 1, 0), pltpu.roll(value, 1, 0)
        )
        beside = beside + jnp.where(
            sub == 7, pltpu.roll(yz[1], 7, 0), pltpu.roll(value, 7, 0)
        )
        spot = lane // 2 % 8
        beside = beside + jnp.where(
            spot == 0, pltpu.roll(xz[0], PART - 14, 1), pltpu.roll(value, 2, 1)
        )
        beside = beside + jnp.where(
            spot == 7, pltpu.roll(xz[1], 14, 1), pltpu.roll(value, PART - 2, 1)
        )
        image = weight * value - THETA * beside
        in_halo[1, starts[4] : starts[4] + 8, :] = image
        in_halo[1, starts[5] : starts[5] + 8, :] = image

    def send_halo_of(step):
        for c in range(3):
            at = c * 8
            out_halo[step, starts[0] + at : starts[0] + at + 8, :] = tile(step, at)
            out_halo[step, starts[1] + at : starts[1] + at + 8, :] = tile(step, at + 7)
        halo(step, 0).start()
        halo(step, 1).start()
        out_halo[step, starts[2] : starts[3], :] = basis[step][pl.ds(0, FIELDS, stride=8), :]
        out_halo[step, starts[3] : starts[4], :] = basis[step][pl.ds(7, FIELDS, stride=8), :]
        halo(step, 2).start()
        halo(step, 3).start()
        faces = turn_faces([tile(step, n) for n in range(FIELDS)], 0, 0)
        out_halo[step, starts[4] : starts[4] + 8, :] = faces
        out_halo[step, starts[5] : starts[5] + 8, :] = faces
        halo(step, 4).start()
        halo(step, 5).start()

    for step in range(ITERS):
        if step == 0:
            send_wide_halo()
        if step == 2:
            send_halo_of(step)
        for n in range(FIELDS):
            value = tile(step, n)
            beside = jnp.where(sub == 0, 0.0, pltpu.roll(value, 1, 0))
            beside = beside + jnp.where(sub == 7, 0.0, pltpu.roll(value, 7, 0))
            beside = beside + jnp.where(lane == 0, 0.0, pltpu.roll(value, 1, 1))
            beside = beside + jnp.where(lane == PART - 1, 0.0, pltpu.roll(value, PART - 1, 1))
            if n % 8:
                beside = beside + tile(step, n - 1)
            if n % 8 < 7:
                beside = beside + tile(step, n + 1)
            basis[step + 1][n * 8 : (n + 1) * 8, :] = diagonal * value - THETA * beside
        if step == 0:
            moments.append(dot(0, 0))
            drain(wide_in, send_wide, recv_wide).wait_recv()
            image_on_faces()
        if step == 2:
            moments.extend((dot(0, 1), dot(1, 1), dot(1, 2), dot(2, 2)))
            drain(in_halo.at[step], send_halo, recv_halo.at[step]).wait_recv()

        def face(side, at=0, size=8):
            if step == 0:
                if side < 4:
                    return wide_in[side * WIDE + at : side * WIDE + at + size, :]
                return wide_in[4 * WIDE + (side - 4) * 16 : 4 * WIDE + (side - 4) * 16 + 8, :]
            return in_halo[step, starts[side] + at : starts[side] + at + size, :]

        low = face(4) * keep[4]
        high = face(5) * keep[5]
        both = jnp.where(lane % 2 == 0, low, pltpu.roll(high, PART - 2, 1))
        for n in range(FIELDS):
            turned = pltpu.roll(both, (PART - 2 * n) % PART, 1)
            more = jnp.where((lane == 0) | (lane == PART - 1), turned, 0.0)
            row_low = face(2, n, 1) * keep[2]
            row_high = face(3, n, 1) * keep[3]
            more = more + jnp.where(sub == 0, jnp.broadcast_to(row_low, (8, PART)), 0.0)
            more = more + jnp.where(sub == 7, jnp.broadcast_to(row_high, (8, PART)), 0.0)
            at = n // 8 * 8
            if n % 8 == 0:
                more = more + face(0, at) * keep[0]
            if n % 8 == 7:
                more = more + face(1, at) * keep[1]
            basis[step + 1][n * 8 : (n + 1) * 8, :] += more
    moments.append(dot(ITERS - 1, ITERS))

    row = lax.broadcasted_iota(jnp.int32, (1, PART), 1)
    packed = jnp.zeros((1, PART), F32)
    for k, moment in enumerate(moments):
        packed = jnp.where(row == k, moment, packed)

    def all_sum(value, buf, n, turn, steps, slot_of, device_of):
        buf[0] = value

        def copy(d):
            return pltpu.make_async_remote_copy(
                src_ref=buf.at[0],
                dst_ref=buf.at[slot_of(d)],
                send_sem=send_sum.at[turn],
                recv_sem=recv_sum.at[turn],
                device_id=device_of(d),
                device_id_type=MESH,
            )

        for d in steps:
            copy(d).start()
        arrived = drain(buf.at[pl.ds(1, n - 1)], send_sum.at[turn], recv_sum.at[turn])
        arrived.wait_recv()
        return jnp.sum(buf[...], axis=0)

    line_steps = sorted(range(1, NGX), key=lambda d: -min(d, NGX - d))
    packed = all_sum(packed, plane_buf, NP, 0, plane_steps, opposite, plane_at)
    total = all_sum(
        packed,
        line_buf,
        NGX,
        1,
        line_steps,
        lambda d: NGX - d,
        lambda d: on_line(lax.rem(gx + d, NGX)),
    )
    m = [jnp.broadcast_to(total[:, k : k + 1], (1, PART)) for k in range(6)]

    def product(a, b):
        result = None
        for i, left in enumerate(a):
            for j, right in enumerate(b):
                term = left * (right * m[i + j])
                result = term if result is None else result + term
        return result

    unit = jnp.ones((1, PART), F32)
    now = [unit]
    course = [unit]
    taken = []
    norm = m[0]
    for step in range(ITERS):
        image = [SHIFT * course[0]]
        for k in range(1, len(course)):
            image.append(SHIFT * course[k] + (1.0 / THETA) * course[k - 1])
        image.append((1.0 / THETA) * course[-1])
        alpha = norm / product(course, image)
        taken = [
            alpha * g + (taken[k] if k < len(taken) else 0.0) for k, g in enumerate(course)
        ]
        now = [
            (now[k] if k < len(now) else 0.0) - alpha * g for k, g in enumerate(image)
        ]
        if step < ITERS - 1:
            following = product(now, now)
            beta = following / norm
            course = [
                g + (beta * course[k] if k < len(course) else 0.0) for k, g in enumerate(now)
            ]
            norm = following
    for k, g in enumerate(taken + now):
        weights_out[k][...] = g

    for half in range(2):
        region = column_buf.at[pl.ds(0, 8 - half)]
        drain(region, send_one.at[half], recv_one.at[half]).wait_send()
        region = lib.at[half, core, pl.ds(0, NP - 1)]
        drain(region, send_two.at[half], recv_two.at[half]).wait_send()
        three(half, core).wait_send()
    drain(out_halo.at[2], send_halo, recv_halo.at[2]).wait_send()
    drain(wide_in, send_wide, recv_wide).wait_send()
    drain(plane_buf.at[pl.ds(1, NP - 1)], send_sum.at[0], recv_sum.at[0]).wait_send()
    drain(line_buf.at[pl.ds(1, NGX - 1)], send_sum.at[1], recv_sum.at[1]).wait_send()


def per_device(source_field, cell_contrast, point_field, point_class, cell_kind, inverse_blocks):
    vmem = pl.BlockSpec(memory_space=pltpu.VMEM)
    dma = pltpu.SemaphoreType.DMA
    results = pl.pallas_call(
        kernel,
        out_shape=[jax.ShapeDtypeStruct((FIELDS * 8, PART), F32)] * (ITERS + 1)
        + [jax.ShapeDtypeStruct((1, PART), F32)] * (2 * ITERS + 1),
        in_specs=[pl.BlockSpec(memory_space=pltpu.HBM)] * 7,
        out_specs=[vmem] * (3 * ITERS + 2),
        scratch_shapes=[
            pltpu.VMEM(source_field.shape, F32),
            pltpu.VMEM(cell_contrast.shape, BF16),
            pltpu.VMEM(point_field.shape, BF16),
            pltpu.VMEM((1, POINTS), jnp.int32),
            pltpu.VMEM((1, POINTS), jnp.int32),
            pltpu.VMEM((9, TYPES, PART), F32),
            pltpu.VMEM((VOX, VOX), BF16),
            pltpu.VMEM((1, ROW), F32),
            pltpu.VMEM((NZC, 1, ROW), F32),
            pltpu.VMEM((2, 2, NP, 16, SPLIT), BF16),
            pltpu.VMEM((4, POINTS, ROW), F32),
            pltpu.VMEM((ITERS, 4 * FIELDS + 16, PART), F32),
            pltpu.VMEM((ITERS, 4 * FIELDS + 16, PART), F32),
            pltpu.VMEM((4 * WIDE + 16, PART), F32),
            pltpu.VMEM((IN_YZ + 32, PART), F32),
            pltpu.VMEM((NP, 1, PART), F32),
            pltpu.VMEM((NGX, 1, PART), F32),
            dma((7,)),
            dma((2,)),
            dma((2,)),
            dma((2,)),
            dma((2,)),
            dma((2,)),
            dma((2,)),
            dma,
            dma((ITERS,)),
            dma,
            dma,
            dma((2,)),
            dma((2,)),
        ],
        compiler_params=pltpu.CompilerParams(
            collective_id=0, has_side_effects=True, vmem_limit_bytes=40 << 20
        ),
    )(
        *[
            pltpu.with_memory_space_constraint(value, pltpu.HBM)
            for value in (
                source_field,
                cell_contrast,
                point_field,
                point_class.reshape(1, -1),
                cell_kind.reshape(1, -1),
                inverse_blocks.transpose(0, 2, 3, 1, 4).reshape(9, TYPES, VOX),
                jnp.asarray(hartley_table()),
            )
        ]
    )
    shape = source_field.shape
    fields = [field.reshape(shape) for field in results[: ITERS + 1]]
    weights = [weight.reshape(PART) for weight in results[ITERS + 1 :]]
    newton_step = sum(weights[k] * fields[k] for k in range(ITERS))
    residual = sum(weights[ITERS + k] * fields[k] for k in range(ITERS + 1))
    return newton_step, residual


def solution(mesh):
    placed = (
        P(None, "gx", "gy", "gz"),
        P(("gx", "gy", "gz"), None),
        P(None, ("gx", "gy", "gz")),
        P(("gx", "gy", "gz"), None),
        P(("gx", "gy", "gz")),
        P("gx", None, None, None, None),
    )
    return jax.shard_map(
        per_device,
        mesh=mesh,
        in_specs=placed,
        out_specs=(P(None, "gx", "gy", "gz"), P(None, "gx", "gy", "gz")),
        check_vma=False,
    )
```

```python
import functools
import math

import jax
import jax.numpy as jnp
import numpy as np
from jax import lax
from jax.experimental import pallas as pl
from jax.experimental.pallas import tpu as pltpu
from jax.sharding import PartitionSpec as P

CELL = 8
VOX = 512
TYPES = 4
ZP = 8
ITERS = 3
NGX = 32
NZC = 16
NP = 16
OWN = 3
REACH = 4
WIDE = 56
IN_XY = 4 * WIDE + 32
IN_XZ = IN_XY + 4 * 24
IN_YZ = IN_XZ + 32
PART = 128
ROW = 9 * PART
SLAB = ROW + PART
SPLIT = SLAB // 2
POINTS = 128
FIELDS = 24
KERR = 0.1
SHIFT = 7.0
THETA = 2.0**-12

MESH = pl.DeviceIdType.MESH
F32 = jnp.float32
BF16 = jnp.bfloat16


def hartley_table():
    n = np.arange(VOX)
    a, b, c = n // (CELL * CELL), n // CELL % CELL, n % CELL
    phase = (np.outer(a, a) + np.outer(b, b) + np.outer(c, c)) % CELL
    angle = 2.0 * math.pi / CELL * np.arange(CELL)
    values = ((np.cos(angle) + np.sin(angle)) / math.sqrt(VOX)).astype(np.float32)
    values[np.abs(values) < 1e-6] = 0.0
    return values.astype(jnp.bfloat16)[phase]


def kernel(
    source_hbm,
    contrast_hbm,
    point_hbm,
    class_hbm,
    kind_hbm,
    inverse_hbm,
    hartley_hbm,
    level_0,
    level_1,
    level_2,
    level_3,
    weight_0,
    weight_1,
    weight_2,
    weight_3,
    weight_4,
    weight_5,
    weight_6,
    source_ref,
    contrast_ref,
    point_ref,
    class_ref,
    kind_ref,
    inverse_ref,
    hartley_ref,
    slice_buf,
    column_buf,
    lib,
    blocks,
    out_halo,
    in_halo,
    wide_out,
    wide_in,
    plane_buf,
    line_buf,
    load_sems,
    send_one,
    recv_one,
    send_two,
    recv_two,
    send_three,
    recv_three,
    send_halo,
    recv_halo,
    send_wide,
    recv_wide,
    send_sum,
    recv_sum,
):
    gx, gy, gz = lax.axis_index("gx"), lax.axis_index("gy"), lax.axis_index("gz")
    chip, core = gx // 2, gx % 2
    place = gy * 4 + gz
    basis = (level_0, level_1, level_2, level_3)
    weights_out = (weight_0, weight_1, weight_2, weight_3, weight_4, weight_5, weight_6)

    def on_line(target):
        return {"gx": target, "gy": gy, "gz": gz}

    def ring(d):
        return min(d, 4 - d)

    plane_steps = sorted(
        range(1, NP), key=lambda d: (-ring(d // 4) - ring(d % 4), d)
    )

    def plane_at(d):
        return {"gx": gx, "gy": lax.rem(gy + d // 4, 4), "gz": lax.rem(gz + d % 4, 4)}

    def opposite(d):
        return (4 - d // 4) % 4 * 4 + (4 - d % 4) % 4

    barrier = pltpu.get_barrier_semaphore()
    near = [d for reach in range(REACH, 0, -1) for d in (reach, NZC - reach)]

    def chip_at(d):
        return on_line(lax.rem(chip + d, NZC) * 2 + core)

    for d in near:
        pl.semaphore_signal(barrier, inc=1, device_id=chip_at(d), device_id_type=MESH)
    for d in plane_steps:
        pl.semaphore_signal(barrier, inc=1, device_id=plane_at(d), device_id_type=MESH)
    pl.semaphore_signal(
        barrier, inc=1, device_id=on_line(chip * 2 + 1 - core), device_id_type=MESH
    )

    loads = [
        pltpu.make_async_copy(
            inverse_hbm.at[:, :, pl.ds(pl.multiple_of(gz * PART, PART), PART)],
            inverse_ref,
            load_sems.at[0],
        )
    ]
    pairs = (
        (point_hbm, point_ref),
        (class_hbm, class_ref),
        (kind_hbm, kind_ref),
        (contrast_hbm, contrast_ref),
        (hartley_hbm, hartley_ref),
        (source_hbm, source_ref),
    )
    for n, (origin, goal) in enumerate(pairs):
        loads.append(pltpu.make_async_copy(origin, goal, load_sems.at[n + 1]))
    for load in loads:
        load.start()
    loads[0].wait()

    for n in range(9):
        slice_buf[:, n * PART : (n + 1) * PART] = inverse_ref[n, pl.ds(gy, 1), :]
    column_buf[OWN] = slice_buf[...]

    pl.semaphore_wait(barrier, 2 * REACH + NP)

    def one(d):
        return pltpu.make_async_remote_copy(
            src_ref=slice_buf,
            dst_ref=column_buf.at[(OWN - d) % NZC],
            send_sem=send_one.at[0],
            recv_sem=recv_one.at[0],
            device_id=chip_at(d),
            device_id_type=MESH,
        )

    for d in near:
        one(d).start()

    for load in loads[1:]:
        load.wait()
    rows = lax.broadcasted_iota(jnp.int32, (8, POINTS), 0)
    point = point_ref[...].astype(F32)
    packed = jnp.zeros((8, POINTS), F32)
    entries = [point[i : i + 1] for i in range(3)]
    entries += [kind_ref[...].astype(F32), class_ref[...].astype(F32)]
    for i, entry in enumerate(entries):
        packed = jnp.where(rows == i, jnp.broadcast_to(entry, (8, POINTS)), packed)
    columns = packed.T
    base = [columns[:, i : i + 1] for i in range(3)]
    kind = columns[:, 3:4].astype(jnp.int32)
    owner = columns[:, 4:5].astype(jnp.int32)
    away = (owner // 2 - chip + OWN + NZC) % NZC
    key = (away // 8) * 128 + (owner % 2) * 64 + kind * 16 + away % 8
    depth = lax.broadcasted_iota(jnp.int32, (POINTS, 2 * POINTS), 1)
    hot = [(depth == key + 8 * turn).astype(F32).astype(BF16) for turn in range(2)]
    weights = [contrast_ref[:, i * VOX : (i + 1) * VOX].astype(F32) for i in range(3)]

    def spectrum_of(polar):
        return [
            jnp.dot(polar[i], hartley_ref[...], preferred_element_type=F32) for i in range(3)
        ]

    first = spectrum_of([(weights[i] * base[i]).astype(BF16) for i in range(3)])

    def relay(start, goal, count, d):
        return pltpu.make_async_remote_copy(
            src_ref=column_buf.at[pl.ds(start, count)],
            dst_ref=column_buf.at[pl.ds(goal, count)],
            send_sem=send_one.at[1],
            recv_sem=recv_one.at[1],
            device_id=chip_at(d),
            device_id_type=MESH,
        )

    def drain(region, send_sem, recv_sem):
        return pltpu.make_async_remote_copy(
            src_ref=region,
            dst_ref=region,
            send_sem=send_sem,
            recv_sem=recv_sem,
            device_id=on_line(chip * 2 + 1 - core),
            device_id_type=MESH,
        )

    def two(half, d):
        at = lib.at[half, core, place]
        return pltpu.make_async_remote_copy(
            src_ref=at,
            dst_ref=at,
            send_sem=send_two.at[half],
            recv_sem=recv_two.at[half],
            device_id=plane_at(d),
            device_id_type=MESH,
        )

    def three(half, which):
        return drain(lib.at[half, which], send_three.at[half], recv_three.at[half])

    lanes = lax.broadcasted_iota(jnp.int32, (8, PART), 1)
    for half in range(2):
        taken = drain(column_buf.at[pl.ds(0, 8 - half)], send_one.at[half], recv_one.at[half])
        taken.wait_recv()
        if half == 0:
            relay(4, 8, 4, NZC - REACH).start()
            relay(0, 12, 3, REACH).start()
        wide = column_buf[half * 8 : (half + 1) * 8].reshape(8, ROW)
        rest = wide - wide.astype(BF16).astype(F32)
        tail = jnp.zeros((8, PART), F32)
        for n in range(9):
            lead = jnp.broadcast_to(rest[:, n * PART : n * PART + 1], (8, PART))
            tail = jnp.where(lanes == n, lead, tail)
        ends = jnp.concatenate([wide[:, SPLIT:ROW], tail], axis=1)
        pair = jnp.concatenate([wide[:, 0:SPLIT], ends], axis=0)
        lib[half, core, place] = pair.astype(BF16)
        for d in plane_steps:
            two(half, d).start()

    for half in range(2):
        region = lib.at[half, core, pl.ds(0, NP - 1)]
        drain(region, send_two.at[half], recv_two.at[half]).wait_recv()
        three(half, core).start()
    for half in range(2):
        three(half, 1 - core).wait_recv()

    for f in range(4):
        part = jnp.concatenate(
            [lib[half, c, k * 4 + f] for half in range(2) for c in range(2) for k in range(4)],
            axis=0,
        )
        chosen = jnp.concatenate(
            [jnp.dot(pick, part, preferred_element_type=F32) for pick in hot], axis=1
        )
        if f:
            blocks[f] = chosen[:, 0:ROW]
        else:
            lead = lax.broadcasted_iota(jnp.int32, (POINTS, PART), 1) == 0
            for n in range(9):
                tail = jnp.broadcast_to(chosen[:, ROW + n : ROW + n + 1], (POINTS, PART))
                blocks[f, :, n * PART : (n + 1) * PART] = chosen[
                    :, n * PART : (n + 1) * PART
                ] + jnp.where(lead, tail, 0.0)

    def correction(spectrum):
        mixed = []
        for i in range(3):
            parts = []
            for f in range(4):
                total = None
                for j in range(3):
                    at = (i * 3 + j) * PART
                    term = (
                        blocks[f, :, at : at + PART]
                        * spectrum[j][:, f * PART : (f + 1) * PART]
                    )
                    total = term if total is None else total + term
                parts.append(total.astype(BF16))
            mixed.append(jnp.concatenate(parts, axis=1))
        return spectrum_of(mixed)

    local = [base[i] - c for i, c in enumerate(correction(first))]
    polar = [
        (weights[i] * local[i] * (1.0 + KERR * local[i] * local[i])).astype(BF16)
        for i in range(3)
    ]
    final = [base[i] - c for i, c in enumerate(correction(spectrum_of(polar)))]
    flux = [
        jnp.sum((1.0 + weights[i]) * final[i], axis=1, keepdims=True) * (1.0 / VOX)
        for i in range(3)
    ]
    energy = sum(weights[i] * final[i] * final[i] for i in range(3))
    stiff = 0.5 + jnp.sum(energy, axis=1, keepdims=True) * (1.0 / (3 * VOX))

    q = lax.broadcasted_iota(jnp.int32, (POINTS, PART), 0)
    z = lax.broadcasted_iota(jnp.int32, (POINTS, PART), 1)
    here = (q % 16) == (z // ZP)

    def to_plane(column):
        spread = jnp.where(here, jnp.broadcast_to(column, (POINTS, PART)), 0.0)
        return jnp.sum(spread.reshape(8, 16, PART), axis=1)

    diagonal = (to_plane(stiff) + (6.0 - SHIFT)) * THETA
    for c in range(3):
        plane = to_plane(flux[c])
        for x in range(8):
            basis[0][(c * 8 + x) * 8 : (c * 8 + x + 1) * 8, :] = source_ref[c, x] - plane

    lane = lax.broadcasted_iota(jnp.int32, (8, PART), 1)
    sub = lax.broadcasted_iota(jnp.int32, (8, PART), 0)
    sides = (
        on_line(lax.rem(gx + NGX - 1, NGX)),
        on_line(lax.rem(gx + 1, NGX)),
        {"gx": gx, "gy": lax.rem(gy + 3, 4), "gz": gz},
        {"gx": gx, "gy": lax.rem(gy + 1, 4), "gz": gz},
        {"gx": gx, "gy": gy, "gz": lax.rem(gz + 3, 4)},
        {"gx": gx, "gy": gy, "gz": lax.rem(gz + 1, 4)},
    )
    starts = (0, FIELDS, 2 * FIELDS, 3 * FIELDS, 4 * FIELDS, 4 * FIELDS + 8)
    sizes = (FIELDS, FIELDS, FIELDS, FIELDS, 8, 8)

    def halo(step, side):
        goal = side + 1 - 2 * (side % 2)
        return pltpu.make_async_remote_copy(
            src_ref=out_halo.at[step, pl.ds(starts[side], sizes[side])],
            dst_ref=in_halo.at[step, pl.ds(starts[goal], sizes[goal])],
            send_sem=send_halo,
            recv_sem=recv_halo.at[step],
            device_id=sides[side],
            device_id_type=MESH,
        )

    def tile(level, n):
        return basis[level][n * 8 : (n + 1) * 8, :]

    def dot(a, b):
        total = tile(a, 0) * tile(b, 0)
        for n in range(1, FIELDS):
            total = total + tile(a, n) * tile(b, n)
        return jnp.sum(jnp.sum(total, axis=0, keepdims=True), axis=1, keepdims=True)

    keep = [
        jnp.where(edge, 0.0, -THETA)
        for edge in (gx == 0, gx == NGX - 1, gy == 0, gy == 3, gz == 0, gz == 3)
    ]
    moments = []

    def around(dx, dy, dz):
        return {
            "gx": lax.rem(gx + dx + NGX, NGX),
            "gy": lax.rem(gy + dy + 4, 4),
            "gz": lax.rem(gz + dz + 4, 4),
        }

    ends = (-1, 1)
    inside = [
        [jnp.where(edge, 0.0, 1.0) for edge in pair]
        for pair in ((gx == 0, gx == NGX - 1), (gy == 0, gy == 3), (gz == 0, gz == 3))
    ]

    def turn_faces(values, first, last):
        faces = jnp.zeros((8, PART), F32)
        for n, value in enumerate(values):
            at_low = pltpu.roll(value, (2 * n + 1 + last) % PART, 1)
            at_high = at_low
            if first or last:
                at_high = pltpu.roll(value, (2 * n + 1 - first) % PART, 1)
            faces = jnp.where(lane == 2 * n, at_low, jnp.where(lane == 2 * n + 1, at_high, faces))
        return faces

    def start_wide(group):
        rows, lines, edges, faces = [], [], [], []
        for e in range(2):
            o = 1 - e
            lines.append((e * WIDE, WIDE, o * WIDE, around(ends[e], 0, 0)))
            lines.append(((2 + e) * WIDE, WIDE, (2 + o) * WIDE, around(0, ends[e], 0)))
            faces.append((4 * WIDE, 16, 4 * WIDE + 16 * o, around(0, 0, ends[e])))
        for e in range(2):
            for g in range(2):
                slot = (1 - e) * 2 + 1 - g
                rows.append(
                    ((2 + g) * WIDE, FIELDS, IN_XY + slot * FIELDS, around(ends[e], ends[g], 0))
                )
                edges.append((4 * WIDE, 8, IN_XZ + slot * 8, around(ends[e], 0, ends[g])))
                edges.append((4 * WIDE, 8, IN_YZ + slot * 8, around(0, ends[e], ends[g])))
        for origin, size, goal, target in (rows, lines, edges, faces)[group]:
            pltpu.make_async_remote_copy(
                src_ref=wide_out.at[pl.ds(origin, size)],
                dst_ref=wide_in.at[pl.ds(goal, size)],
                send_sem=send_wide,
                recv_sem=recv_wide,
                device_id=target,
                device_id_type=MESH,
            ).start()

    def send_wide_halo():
        for e, (near_y, next_y) in enumerate(((0, 1), (7, 6))):
            at = (2 + e) * WIDE
            wide_out[at : at + 24, :] = basis[0][pl.ds(near_y, FIELDS, stride=8), :]
            wide_out[at + 24 : at + 48, :] = basis[0][pl.ds(next_y, FIELDS, stride=8), :]
            wide_out[at + 48 : at + 56, :] = jnp.broadcast_to(
                diagonal[near_y : near_y + 1], (8, PART)
            )
        start_wide(0)
        for e, (near_x, next_x) in enumerate(((0, 1), (7, 6))):
            at = e * WIDE
            for c in range(3):
                wide_out[at + c * 8 : at + c * 8 + 8, :] = tile(0, c * 8 + near_x)
                wide_out[at + 24 + c * 8 : at + 32 + c * 8, :] = tile(0, c * 8 + next_x)
            wide_out[at + 48 : at + 56, :] = diagonal
        start_wide(1)
        values = [tile(0, n) for n in range(FIELDS)]
        wide_out[4 * WIDE : 4 * WIDE + 8, :] = turn_faces(values + [diagonal], 0, 0)
        start_wide(2)
        wide_out[4 * WIDE + 8 : 4 * WIDE + 16, :] = turn_faces(values, 1, 1)
        start_wide(3)

    def spread_row(value):
        return jnp.broadcast_to(value, (8, PART))

    def image_on_faces():
        even = lane % 2 == 0

        def part(at, size=8):
            return wide_in[at : at + size, :]

        def corner_rows(e, g, n):
            at = IN_XY + (e * 2 + g) * FIELDS + n
            return wide_in[at : at + 1, :] * inside[0][e] * inside[1][g]

        def mixed(at, low, high):
            return jnp.where(even, part(at) * low, part(at + 8) * high)

        xz = [mixed(IN_XZ + 16 * e, *inside[2]) * inside[0][e] for e in range(2)]
        yz = [mixed(IN_YZ + 16 * e, *inside[2]) * inside[1][e] for e in range(2)]
        for e in range(2):
            n_at = 7 if e == 0 else 0
            at = e * WIDE
            own_x = 0 if e == 0 else 7
            for c in range(3):
                value = part(at + c * 8)
                n = c * 8 + n_at
                beside = part(at + 24 + c * 8) + tile(0, c * 8 + own_x)
                beside = beside + jnp.where(
                    sub == 0, spread_row(corner_rows(e, 0, n)), pltpu.roll(value, 1, 0)
                )
                beside = beside + jnp.where(
                    sub == 7, spread_row(corner_rows(e, 1, n)), pltpu.roll(value, 7, 0)
                )
                beside = beside + jnp.where(
                    lane == 0,
                    pltpu.roll(xz[e], (PART - 2 * n) % PART, 1),
                    pltpu.roll(value, 1, 1),
                )
                beside = beside + jnp.where(
                    lane == PART - 1,
                    pltpu.roll(xz[e], (PART - 2 - 2 * n) % PART, 1),
                    pltpu.roll(value, PART - 1, 1),
                )
                image = part(at + 48) * value - THETA * beside
                goal = starts[e] + c * 8
                in_halo[1, goal : goal + 8, :] = image * inside[0][e]
            at = (2 + e) * WIDE
            row_at = 7 if e == 0 else 0
            edge = spread_row(yz[e][row_at : row_at + 1])
            for c in range(3):
                value = part(at + c * 8)
                own = wide_out[at + c * 8 : at + c * 8 + 8, :]
                beside = part(at + 24 + c * 8) + own
                beside = beside + jnp.where(
                    sub == 0, spread_row(corner_rows(0, e, c * 8 + 7)), pltpu.roll(value, 1, 0)
                )
                beside = beside + jnp.where(
                    sub == 7, spread_row(corner_rows(1, e, c * 8)), pltpu.roll(value, 7, 0)
                )
                lanes_low = 2 * (c * 8 + sub)
                low = jnp.sum(jnp.where(lane == lanes_low, edge, 0.0), axis=1, keepdims=True)
                high = jnp.sum(jnp.where(lane == lanes_low + 1, edge, 0.0), axis=1, keepdims=True)
                beside = beside + jnp.where(
                    lane == 0, jnp.broadcast_to(low, (8, PART)), pltpu.roll(value, 1, 1)
                )
                beside = beside + jnp.where(
                    lane == PART - 1,
                    jnp.broadcast_to(high, (8, PART)),
                    pltpu.roll(value, PART - 1, 1),
                )
                image = part(at + 48) * value - THETA * beside
                goal = starts[2 + e] + c * 8
                in_halo[1, goal : goal + 8, :] = image * inside[1][e]
        at = 4 * WIDE
        value = jnp.where(even, part(at), part(at + 16))
        beyond = jnp.where(even, part(at + 8), part(at + 24))
        faces = wide_out[at : at + 8, :]
        own = jnp.where(even, pltpu.roll(faces, PART - 1, 1), pltpu.roll(faces, 1, 1))
        weight = jnp.where(
            even,
            jnp.broadcast_to(part(at)[:, 48:49], (8, PART)),
            jnp.broadcast_to(part(at + 16)[:, 49:50], (8, PART)),
        )
        beside = beyond + own
        beside = beside + jnp.where(
            sub == 0, pltpu.roll(yz[0], 1, 0), pltpu.roll(value, 1, 0)
        )
        beside = beside + jnp.where(
            sub == 7, pltpu.roll(yz[1], 7, 0), pltpu.roll(value, 7, 0)
        )
        spot = lane // 2 % 8
        beside = beside + jnp.where(
            spot == 0, pltpu.roll(xz[0], PART - 14, 1), pltpu.roll(value, 2, 1)
        )
        beside = beside + jnp.where(
            spot == 7, pltpu.roll(xz[1], 14, 1), pltpu.roll(value, PART - 2, 1)
        )
        image = weight * value - THETA * beside
        in_halo[1, starts[4] : starts[4] + 8, :] = image
        in_halo[1, starts[5] : starts[5] + 8, :] = image

    def send_halo_of(step):
        for c in range(3):
            at = c * 8
            out_halo[step, starts[0] + at : starts[0] + at + 8, :] = tile(step, at)
            out_halo[step, starts[1] + at : starts[1] + at + 8, :] = tile(step, at + 7)
        halo(step, 0).start()
        halo(step, 1).start()
        out_halo[step, starts[2] : starts[3], :] = basis[step][pl.ds(0, FIELDS, stride=8), :]
        out_halo[step, starts[3] : starts[4], :] = basis[step][pl.ds(7, FIELDS, stride=8), :]
        halo(step, 2).start()
        halo(step, 3).start()
        faces = turn_faces([tile(step, n) for n in range(FIELDS)], 0, 0)
        out_halo[step, starts[4] : starts[4] + 8, :] = faces
        out_halo[step, starts[5] : starts[5] + 8, :] = faces
        halo(step, 4).start()
        halo(step, 5).start()

    for step in range(ITERS):
        if step == 0:
            send_wide_halo()
        if step == 2:
            send_halo_of(step)
        for n in range(FIELDS):
            value = tile(step, n)
            beside = jnp.where(sub == 0, 0.0, pltpu.roll(value, 1, 0))
            beside = beside + jnp.where(sub == 7, 0.0, pltpu.roll(value, 7, 0))
            beside = beside + jnp.where(lane == 0, 0.0, pltpu.roll(value, 1, 1))
            beside = beside + jnp.where(lane == PART - 1, 0.0, pltpu.roll(value, PART - 1, 1))
            if n % 8:
                beside = beside + tile(step, n - 1)
            if n % 8 < 7:
                beside = beside + tile(step, n + 1)
            basis[step + 1][n * 8 : (n + 1) * 8, :] = diagonal * value - THETA * beside
        if step == 0:
            moments.append(dot(0, 0))
            drain(wide_in, send_wide, recv_wide).wait_recv()
            image_on_faces()
        if step == 2:
            moments.extend((dot(0, 1), dot(1, 1), dot(1, 2), dot(2, 2)))
            drain(in_halo.at[step], send_halo, recv_halo.at[step]).wait_recv()

        def face(side, at=0, size=8):
            if step == 0:
                if side < 4:
                    return wide_in[side * WIDE + at : side * WIDE + at + size, :]
                return wide_in[4 * WIDE + (side - 4) * 16 : 4 * WIDE + (side - 4) * 16 + 8, :]
            return in_halo[step, starts[side] + at : starts[side] + at + size, :]

        low = face(4) * keep[4]
        high = face(5) * keep[5]
        both = jnp.where(lane % 2 == 0, low, pltpu.roll(high, PART - 2, 1))
        for n in range(FIELDS):
            turned = pltpu.roll(both, (PART - 2 * n) % PART, 1)
            more = jnp.where((lane == 0) | (lane == PART - 1), turned, 0.0)
            row_low = face(2, n, 1) * keep[2]
            row_high = face(3, n, 1) * keep[3]
            more = more + jnp.where(sub == 0, jnp.broadcast_to(row_low, (8, PART)), 0.0)
            more = more + jnp.where(sub == 7, jnp.broadcast_to(row_high, (8, PART)), 0.0)
            at = n // 8 * 8
            if n % 8 == 0:
                more = more + face(0, at) * keep[0]
            if n % 8 == 7:
                more = more + face(1, at) * keep[1]
            basis[step + 1][n * 8 : (n + 1) * 8, :] += more
    moments.append(dot(ITERS - 1, ITERS))

    row = lax.broadcasted_iota(jnp.int32, (1, PART), 1)
    packed = jnp.zeros((1, PART), F32)
    for k, moment in enumerate(moments):
        packed = jnp.where(row == k, moment, packed)

    def all_sum(value, buf, n, turn, steps, slot_of, device_of):
        buf[0] = value

        def copy(d):
            return pltpu.make_async_remote_copy(
                src_ref=buf.at[0],
                dst_ref=buf.at[slot_of(d)],
                send_sem=send_sum.at[turn],
                recv_sem=recv_sum.at[turn],
                device_id=device_of(d),
                device_id_type=MESH,
            )

        for d in steps:
            copy(d).start()
        arrived = drain(buf.at[pl.ds(1, n - 1)], send_sum.at[turn], recv_sum.at[turn])
        arrived.wait_recv()
        return jnp.sum(buf[...], axis=0)

    line_steps = sorted(range(1, NGX), key=lambda d: -min(d, NGX - d))
    packed = all_sum(
        packed,
        line_buf,
        NGX,
        1,
        line_steps,
        lambda d: NGX - d,
        lambda d: on_line(lax.rem(gx + d, NGX)),
    )
    total = all_sum(packed, plane_buf, NP, 0, plane_steps, opposite, plane_at)
    m = [jnp.broadcast_to(total[:, k : k + 1], (1, PART)) for k in range(6)]

    def product(a, b):
        result = None
        for i, left in enumerate(a):
            for j, right in enumerate(b):
                term = left * (right * m[i + j])
                result = term if result is None else result + term
        return result

    unit = jnp.ones((1, PART), F32)
    now = [unit]
    course = [unit]
    taken = []
    norm = m[0]
    for step in range(ITERS):
        image = [SHIFT * course[0]]
        for k in range(1, len(course)):
            image.append(SHIFT * course[k] + (1.0 / THETA) * course[k - 1])
        image.append((1.0 / THETA) * course[-1])
        alpha = norm / product(course, image)
        taken = [
            alpha * g + (taken[k] if k < len(taken) else 0.0) for k, g in enumerate(course)
        ]
        now = [
            (now[k] if k < len(now) else 0.0) - alpha * g for k, g in enumerate(image)
        ]
        if step < ITERS - 1:
            following = product(now, now)
            beta = following / norm
            course = [
                g + (beta * course[k] if k < len(course) else 0.0) for k, g in enumerate(now)
            ]
            norm = following
    for k, g in enumerate(taken + now):
        weights_out[k][...] = g

    for half in range(2):
        region = column_buf.at[pl.ds(0, 8 - half)]
        drain(region, send_one.at[half], recv_one.at[half]).wait_send()
        region = lib.at[half, core, pl.ds(0, NP - 1)]
        drain(region, send_two.at[half], recv_two.at[half]).wait_send()
        three(half, core).wait_send()
    drain(out_halo.at[2], send_halo, recv_halo.at[2]).wait_send()
    drain(wide_in, send_wide, recv_wide).wait_send()
    drain(plane_buf.at[pl.ds(1, NP - 1)], send_sum.at[0], recv_sum.at[0]).wait_send()
    drain(line_buf.at[pl.ds(1, NGX - 1)], send_sum.at[1], recv_sum.at[1]).wait_send()


def per_device(source_field, cell_contrast, point_field, point_class, cell_kind, inverse_blocks):
    vmem = pl.BlockSpec(memory_space=pltpu.VMEM)
    dma = pltpu.SemaphoreType.DMA
    results = pl.pallas_call(
        kernel,
        out_shape=[jax.ShapeDtypeStruct((FIELDS * 8, PART), F32)] * (ITERS + 1)
        + [jax.ShapeDtypeStruct((1, PART), F32)] * (2 * ITERS + 1),
        in_specs=[pl.BlockSpec(memory_space=pltpu.HBM)] * 7,
        out_specs=[vmem] * (3 * ITERS + 2),
        scratch_shapes=[
            pltpu.VMEM(source_field.shape, F32),
            pltpu.VMEM(cell_contrast.shape, BF16),
            pltpu.VMEM(point_field.shape, BF16),
            pltpu.VMEM((1, POINTS), jnp.int32),
            pltpu.VMEM((1, POINTS), jnp.int32),
            pltpu.VMEM((9, TYPES, PART), F32),
            pltpu.VMEM((VOX, VOX), BF16),
            pltpu.VMEM((1, ROW), F32),
            pltpu.VMEM((NZC, 1, ROW), F32),
            pltpu.VMEM((2, 2, NP, 16, SPLIT), BF16),
            pltpu.VMEM((4, POINTS, ROW), F32),
            pltpu.VMEM((ITERS, 4 * FIELDS + 16, PART), F32),
            pltpu.VMEM((ITERS, 4 * FIELDS + 16, PART), F32),
            pltpu.VMEM((4 * WIDE + 16, PART), F32),
            pltpu.VMEM((IN_YZ + 32, PART), F32),
            pltpu.VMEM((NP, 1, PART), F32),
            pltpu.VMEM((NGX, 1, PART), F32),
            dma((7,)),
            dma((2,)),
            dma((2,)),
            dma((2,)),
            dma((2,)),
            dma((2,)),
            dma((2,)),
            dma,
            dma((ITERS,)),
            dma,
            dma,
            dma((2,)),
            dma((2,)),
        ],
        compiler_params=pltpu.CompilerParams(
            collective_id=0, has_side_effects=True, vmem_limit_bytes=40 << 20
        ),
    )(
        *[
            pltpu.with_memory_space_constraint(value, pltpu.HBM)
            for value in (
                source_field,
                cell_contrast,
                point_field,
                point_class.reshape(1, -1),
                cell_kind.reshape(1, -1),
                inverse_blocks.transpose(0, 2, 3, 1, 4).reshape(9, TYPES, VOX),
                jnp.asarray(hartley_table()),
            )
        ]
    )
    shape = source_field.shape
    fields = [field.reshape(shape) for field in results[: ITERS + 1]]
    weights = [weight.reshape(PART) for weight in results[ITERS + 1 :]]
    newton_step = sum(weights[k] * fields[k] for k in range(ITERS))
    residual = sum(weights[ITERS + k] * fields[k] for k in range(ITERS + 1))
    return newton_step, residual


def solution(mesh):
    placed = (
        P(None, "gx", "gy", "gz"),
        P(("gx", "gy", "gz"), None),
        P(None, ("gx", "gy", "gz")),
        P(("gx", "gy", "gz"), None),
        P(("gx", "gy", "gz")),
        P("gx", None, None, None, None),
    )
    return jax.shard_map(
        per_device,
        mesh=mesh,
        in_specs=placed,
        out_specs=(P(None, "gx", "gy", "gz"), P(None, "gx", "gy", "gz")),
        check_vma=False,
    )
```
